256 devices in a mesh: dp: 8 (over x, z_lo), seq: 32 (over z_hi, y, core).
Axes of the slice: x: 4, y: 4, z: 8 (z_hi: 4, z_lo: 2; z = z_hi * 2 + z_lo), core: 2. Of those that a mesh axis runs over, the one named last changes fastest.
Arguments:
- tower_grad: bfloat16 [8192, 768], P(None, ('dp', 'seq')), may hold values from -6 to 6
- act_mid: bfloat16 [16384, 704], P('seq'), may hold values from -6 to 6
- pre_mid: bfloat16 [16384, 768], P('seq', 'dp'), may hold values from -6 to 6
- act_low: bfloat16 [32768, 640], P('seq'), may hold values from -6 to 6
- pre_low: bfloat16 [32768, 704], P('seq', 'dp'), may hold values from -6 to 6
- weight_upper: bfloat16 [5, 704, 768], P(None, 'seq', 'dp'), may hold values from -0.109375 to 0.109375
- weight_lower: bfloat16 [5, 640, 704], P(None, 'seq', 'dp'), may hold values from -0.109375 to 0.109375
Outputs:
- grad_low_act: bfloat16 [32768, 640], P('seq', 'dp')
- grad_upper: float32 [5, 704, 768], P(None, 'seq', 'dp')
- grad_lower: float32 [5, 640, 704], P(None, 'seq', 'dp')
The draws below stay inside these ranges and needn't reach their ends.
All inputs are finite; a program needn't handle non-finite values.
Results may differ from the reference program's by a relative error of at most 0.0065.
Values may be sent and summed in bfloat16 or wider, within the bound.
No kernel may reach another device: no remote copies, remote signals or barrier semaphores. Data moves between devices by JAX's collectives and lax.ppermute only.
A program may use at most 64 MiB of HBM per device.

```python
import math
import jax
import jax.numpy as jnp
from jax import lax

CH_TOP = 768
CH_MID = 704
CH_LOW = 640
KWIDTH = 5
TOP = 8192
MID = 16384
LOW = 32768


def with_spikes(result, own_key, source, target, blocks, factor):
    def block_of(dim):
        return (jnp.arange(result.shape[dim]) // (result.shape[dim] // blocks)).reshape((-1,) + (1,) * (result.ndim - 1 - dim))

    first = jax.random.permutation(own_key, blocks)[block_of(target)]
    far = (block_of(target) + blocks // 2) % blocks
    return jnp.where((block_of(source) == first) | (block_of(source) == far), factor * result, result)


def block_levels(stream_key, dims, shards, least, high):
    def one(axis_at, blocks):
        heights = jax.random.uniform(jax.random.fold_in(jax.random.fold_in(stream_key, 6), axis_at), (blocks,), jnp.float32, least / len(shards), high / len(shards))
        return jnp.repeat(jnp.exp(heights), dims[axis_at] // blocks).reshape((-1,) + (1,) * (len(dims) - axis_at - 1))

    factor_of = one(*shards[0])
    for cut in shards[1:]:
        factor_of = factor_of * one(*cut)
    return factor_of


def normal_values(key, dims, deviation, bound, cuts=(), held_as=jnp.bfloat16):
    values = jax.random.normal(key, dims, jnp.float32) * deviation
    if len(cuts) > 0:
        values = block_levels(key, dims, cuts, -0.22, 0.18) * values
    return jnp.clip(values, min=-bound, max=bound).astype(held_as)


def gaussian_with(rng, dims, scale, reach, cuts, heavy, dtype=jnp.bfloat16):
    result = scale * jax.random.normal(rng, dims, jnp.float32)
    if cuts:
        result = result * block_levels(rng, dims, cuts, -0.22, 0.18)
    return jnp.clip(with_spikes(result, jax.random.fold_in(rng, 3), *heavy), -reach, reach).astype(dtype)


def setup_inputs(seed: int = 0) -> dict:
    splits = jax.random.split(jax.random.key(seed), 8)
    return {
        "tower_grad": normal_values(splits[0], (TOP, CH_TOP), 1.0, 6.0, ((1, 256),)),
        "act_mid": gaussian_with(splits[1], (MID, CH_MID), 1.0, 6.0, ((0, 32),), (0, 1, 32, 2.75)),
        "pre_mid": normal_values(splits[2], (MID, CH_TOP), 1.5, 6.0, ((0, 32), (1, 8))),
        "act_low": gaussian_with(splits[3], (LOW, CH_LOW), 1.0, 6.0, ((0, 32),), (0, 1, 32, 2.75)),
        "pre_low": normal_values(splits[4], (LOW, CH_MID), 1.5, 6.0, ((0, 32), (1, 8))),
        "weight_upper": normal_values(splits[5], (KWIDTH, CH_MID, CH_TOP), (KWIDTH * CH_MID) ** -0.5, 0.109375, ((1, 32), (2, 8))),
        "weight_lower": normal_values(splits[6], (KWIDTH, CH_LOW, CH_MID), (KWIDTH * CH_LOW) ** -0.5, 0.109375, ((1, 32), (2, 8))),
    }


def gelu_slope(pre_act):
    values = pre_act.astype(jnp.float32)
    cumulative = 0.5 * (1.0 + lax.erf(values * (1.0 / math.sqrt(2.0))))
    density = jnp.exp(-0.5 * values * values) * (1.0 / math.sqrt(2.0 * math.pi))
    return cumulative + values * density

def level_back(upper_grad, act, pre_act, weight):
    rows = act.shape[0]
    half = KWIDTH // 2
    spread = jnp.repeat(upper_grad.astype(jnp.float32), 2, axis=0) * 0.5
    pre_grad = (spread * gelu_slope(pre_act)).astype(jnp.bfloat16)
    padded = jnp.pad(pre_grad, ((half, half), (0, 0)))
    act_grad = jnp.zeros((rows, weight.shape[1]), jnp.float32)
    pieces = []
    for offset in range(KWIDTH):
        begin = 2 * half - offset
        shifted = padded[begin:begin + rows]
        pieces.append(jnp.dot(act.T, shifted, preferred_element_type=jnp.float32))
        act_grad = act_grad + jnp.dot(shifted, weight[offset].T, preferred_element_type=jnp.float32)
    return (act_grad, jnp.stack(pieces))

def reference(tower_grad, act_mid, pre_mid, act_low, pre_low, weight_upper, weight_lower):
    mid_grad, upper_part = level_back(tower_grad, act_mid, pre_mid, weight_upper)
    low_grad, lower_part = level_back(mid_grad.astype(jnp.bfloat16), act_low, pre_low, weight_lower)
    grad_upper = upper_part * (1.0 / math.sqrt(MID))
    grad_lower = lower_part * (1.0 / math.sqrt(LOW))
    return (low_grad.astype(jnp.bfloat16), grad_upper, grad_lower)
```

```python
import math

import jax
import jax.numpy as jnp
from jax import lax
from jax.experimental import pallas as pl
from jax.experimental.pallas import tpu as pltpu
from jax.sharding import Mesh, PartitionSpec as P

KWIDTH = 5
HALF = 2
DP = ("x", "zl")
SEQ = ("zh", "y", "c")
NZ, NY, NC = 4, 4, 2
BF = jnp.bfloat16
F32 = jnp.float32
PARAMS = pltpu.CompilerParams(vmem_limit_bytes=40 * 1024 * 1024)
VMEM = pl.BlockSpec(memory_space=pltpu.VMEM)
SMEM = pl.BlockSpec(memory_space=pltpu.SMEM)


def half_slope(pre_act):
    values = pre_act.astype(F32)
    cumulative = 0.5 * (1.0 + lax.erf(values * (1.0 / math.sqrt(2.0))))
    density = jnp.exp(-0.5 * values * values) * (1.0 / math.sqrt(2.0 * math.pi))
    return 0.5 * (cumulative + values * density)


def shifted(block, axis, count, step):
    return lax.ppermute(block, axis, [(i, (i + step) % count) for i in range(count)])


def gather_rows(block):
    level = jnp.stack([block] + [shifted(block, "zh", NZ, s) for s in range(1, NZ)])
    level = jnp.concatenate([level] + [shifted(level, "y", NY, s) for s in range(1, NY)])
    return level, shifted(level, "c", NC, 1)


def scatter_rows(keep, send):
    total = keep + shifted(send, "c", NC, 1).astype(F32)
    parts = [shifted(total[s].astype(BF), "y", NY, s) for s in range(1, NY)]
    total = total[0] + sum(p.astype(F32) for p in parts)
    parts = [shifted(total[s].astype(BF), "zh", NZ, s) for s in range(1, NZ)]
    return total[0] + sum(p.astype(F32) for p in parts)


def source_slot(q, pos):
    zh, y = q // (NY * NC), (q // NC) % NY
    return lax.rem(pos[1] - y + NY, NY) * NZ + lax.rem(pos[0] - zh + NZ, NZ)


def block_of(q, pos, own_ref, other_ref):
    slot = source_slot(q, pos)
    mine = own_ref[slot].astype(F32)
    theirs = other_ref[slot].astype(F32)
    return jnp.where(pos[2] == q % NC, mine, theirs)


def doubling():
    row = lax.broadcasted_iota(jnp.int32, (128, 256), 0)
    col = lax.broadcasted_iota(jnp.int32, (128, 256), 1)
    return (row == lax.shift_right_logical(col, 1)).astype(F32).astype(BF)


def mm(a, b):
    return jnp.dot(a, b, preferred_element_type=F32)


def upper_kernel(pos_ref, tower_ref, slope_ref, own_ref, other_ref, mid_ref, taps_ref, main_ref, edge_ref, w_ref):
    pos = (pos_ref[0], pos_ref[1], pos_ref[2])
    for q in range(32):
        rows = tower_ref[q].astype(F32)
        main_ref[3 * q : 3 * q + 3, :] = rows[0:3]
        edge_ref[3 * q : 3 * q + 3, :] = rows[3:6]
    for pair in range(16):
        both = [block_of(2 * pair + j, pos, own_ref, other_ref) for j in range(2)]
        w_ref[48 * pair : 48 * pair + 48, :] = jnp.concatenate(both, axis=0).astype(BF)
    spread = doubling()
    main = main_ref[...].astype(BF)
    edge = edge_ref[...].astype(BF)
    grad = jnp.concatenate(
        [
            mm(edge[:, :128], spread)[:, 128:],
            mm(main[:, :128], spread),
            mm(main[:, 128:], spread),
            mm(edge[:, 128:], spread)[:, :128],
        ],
        axis=1,
    )
    grad = grad * slope_ref[...]
    lane = lax.broadcasted_iota(jnp.int32, (96, 128), 1)
    for k in range(KWIDTH):
        moved = pltpu.roll(grad, 768 - (130 - k), 1)
        outer = jnp.where(lane == 127, moved[:, 640:768], moved[:, 512:640])
        taps_ref[96 * k : 96 * k + 96, 0:512] = moved[:, 0:512].astype(BF)
        taps_ref[96 * k : 96 * k + 96, 512:640] = outer.astype(BF)
    taps = taps_ref[...]
    for d in range(8):
        mid_ref[d] = mm(w_ref[96 * d : 96 * d + 96, :], taps).astype(BF)


def lower_weight_kernel(pos_ref, own_ref, other_ref, out_ref, rows_ref):
    pos = (pos_ref[0], pos_ref[1], pos_ref[2])
    for q in range(32):
        rows_ref[20 * q : 20 * q + 24, :] = block_of(q, pos, own_ref, other_ref)
    out_ref[...] = rows_ref[0:640, :].astype(BF)


def lower_kernel(pos_ref, mid_ref, slope_ref, w_ref, low_ref, taps_ref):
    place = pos_ref[0] * (NY * NC) + pos_ref[1] * NC + pos_ref[2]
    total = mid_ref[0].astype(F32)
    for d in range(1, 8):
        total = total + mid_ref[d].astype(F32)
    mid = total.astype(BF)
    ends = mid[:, 512:640].astype(F32)
    left = jnp.broadcast_to(jnp.where(place == 0, 0.0, ends[:, 127:128]), (96, 128))
    right = jnp.broadcast_to(jnp.where(place == 31, 0.0, ends[:, 0:1]), (96, 128))
    spread = doubling()
    grad = jnp.concatenate(
        [left] + [mm(mid[:, 128 * j : 128 * j + 128], spread) for j in range(4)] + [right], axis=1
    )
    grad = grad * slope_ref[...]
    for k in range(KWIDTH):
        moved = pltpu.roll(grad, 1280 - (130 - k), 1)
        taps_ref[96 * k : 96 * k + 96, :] = moved[:, 0:1024].astype(BF)
    taps = taps_ref[...]
    for d in range(8):
        low_ref[d] = mm(w_ref[80 * d : 80 * d + 80, :], taps).astype(BF)


def weight_grad_kernel(pos_ref, act_ref, taps_ref, keep_ref, send_ref, rows_ref, block_ref):
    channels, count = act_ref.shape
    width = channels // 32
    rows_ref[channels:, :] = jnp.zeros((8, rows_ref.shape[1]), F32)
    rows_ref[0:channels, :] = lax.dot_general(
        act_ref[...], taps_ref[:, 0:count], (((1,), (1,)), ((), ())), preferred_element_type=F32
    )
    for q in range(32):
        block_ref[q] = rows_ref[width * q : width * q + 24, :]
    for ry in range(NY):
        for rz in range(NZ):
            zh = lax.rem(pos_ref[0] + rz, NZ)
            y = lax.rem(pos_ref[1] + ry, NY)
            base = (zh * NY + y) * NC
            keep_ref[ry, rz] = block_ref[base + pos_ref[2]]
            send_ref[ry, rz] = block_ref[base + 1 - pos_ref[2]].astype(BF)


def weight_grad(pos, act, taps):
    block = (NY, NZ, 24, taps.shape[0])
    return pl.pallas_call(
        weight_grad_kernel,
        out_shape=(jax.ShapeDtypeStruct(block, F32), jax.ShapeDtypeStruct(block, BF)),
        in_specs=[SMEM, VMEM, VMEM],
        out_specs=(VMEM, VMEM),
        scratch_shapes=[pltpu.VMEM((act.shape[0] + 8, taps.shape[0]), F32), pltpu.VMEM((32, 24, taps.shape[0]), F32)],
        compiler_params=PARAMS,
        name="weight_grad",
    )(pos, act, taps)


def neighbours(block):
    count = NZ * NY * NC
    forward = [(i, i + 1) for i in range(count - 1)]
    backward = [(i + 1, i) for i in range(count - 1)]
    low = lax.ppermute(block[:, :, -128:], SEQ, forward)
    high = lax.ppermute(block[:, :, :128], SEQ, backward)
    return low, high


def local(tower_grad, act_mid, pre_mid, act_low, pre_low, weight_upper, weight_lower):
    pos = jnp.stack([lax.axis_index("zh"), lax.axis_index("y"), lax.axis_index("c")]).astype(jnp.int32)
    tower = tower_grad.T.reshape(3, 32, 256)
    blank = jnp.zeros((3, 1, 128), BF)
    before = jnp.concatenate([blank, tower[:, :-1, 128:]], axis=1)
    after = jnp.concatenate([tower[:, 1:, :128], blank], axis=1)
    windows = jnp.concatenate([tower, jnp.concatenate([before, after], axis=2)], axis=0)
    tower_rows = lax.all_to_all(windows.transpose(1, 0, 2), SEQ, split_axis=0, concat_axis=0, tiled=True)

    upper = jnp.pad(weight_upper.transpose(1, 0, 2).reshape(22, 480), ((0, 2), (0, 0)))
    lower = jnp.pad(weight_lower.reshape(5, 20, 4, 22), ((0, 0), (0, 4), (0, 0), (0, 2)))
    lower = lower.transpose(1, 0, 2, 3).reshape(24, 480)
    upper_own, upper_other = gather_rows(upper)
    lower_own, lower_other = gather_rows(lower)

    pre_upper = pre_mid.T
    pre_lower = jnp.pad(pre_low.T.reshape(4, 22, 1024), ((0, 0), (0, 2), (0, 0))).reshape(96, 1024)
    edges = jnp.stack(
        [
            jnp.concatenate([pre_upper[:, :128], pre_upper[:, -128:]], axis=1),
            jnp.concatenate([pre_lower[:, :128], pre_lower[:, -128:]], axis=1),
        ]
    )
    low_side, high_side = neighbours(edges)
    slope_upper = half_slope(jnp.concatenate([low_side[0], pre_upper, high_side[0]], axis=1))
    slope_lower = half_slope(jnp.concatenate([low_side[1], pre_lower, high_side[1]], axis=1))

    mid_part, upper_taps = pl.pallas_call(
        upper_kernel,
        out_shape=(jax.ShapeDtypeStruct((8, 96, 640), BF), jax.ShapeDtypeStruct((480, 640), BF)),
        in_specs=[SMEM] + [VMEM] * 4,
        out_specs=(VMEM, VMEM),
        scratch_shapes=[pltpu.VMEM((96, 256), F32), pltpu.VMEM((96, 256), F32), pltpu.VMEM((768, 480), BF)],
        compiler_params=PARAMS,
        name="upper",
    )(pos, tower_rows, slope_upper, upper_own.reshape(16, 24, 480), upper_other.reshape(16, 24, 480))
    mid_parts = lax.all_to_all(mid_part, DP, split_axis=0, concat_axis=0, tiled=True)

    upper_sum = scatter_rows(*weight_grad(pos, act_mid.T, upper_taps))
    lower_full = pl.pallas_call(
        lower_weight_kernel,
        out_shape=jax.ShapeDtypeStruct((640, 480), BF),
        in_specs=[SMEM] + [VMEM] * 2,
        out_specs=VMEM,
        scratch_shapes=[pltpu.VMEM((648, 480), F32)],
        compiler_params=PARAMS,
        name="lower_weight",
    )(pos, lower_own.reshape(16, 24, 480), lower_other.reshape(16, 24, 480))

    low_part, lower_taps = pl.pallas_call(
        lower_kernel,
        out_shape=(jax.ShapeDtypeStruct((8, 80, 1024), BF), jax.ShapeDtypeStruct((480, 1024), BF)),
        in_specs=[SMEM] + [VMEM] * 3,
        out_specs=(VMEM, VMEM),
        compiler_params=PARAMS,
        name="lower",
    )(pos, mid_parts, slope_lower, lower_full)
    low_parts = lax.all_to_all(low_part, DP, split_axis=0, concat_axis=0, tiled=True)
    lower_sum = scatter_rows(*weight_grad(pos, act_low.T, lower_taps))

    low_grad = jnp.sum(low_parts.astype(F32), axis=0).astype(BF).T
    mid_total = act_mid.shape[0] * NZ * NY * NC
    low_total = act_low.shape[0] * NZ * NY * NC
    grad_upper = upper_sum[:22].reshape(22, 5, 96).transpose(1, 0, 2) * (1.0 / math.sqrt(mid_total))
    grad_lower = lower_sum[:20].reshape(20, 5, 4, 24)[:, :, :, :22].reshape(20, 5, 88)
    grad_lower = grad_lower.transpose(1, 0, 2) * (1.0 / math.sqrt(low_total))
    return low_grad, grad_upper, grad_lower


def solution(mesh):
    fine = Mesh(mesh.devices.reshape(4, 2, NZ, NY, NC), DP + SEQ)
    in_specs = (
        P(None, DP + SEQ),
        P(SEQ, None),
        P(SEQ, DP),
        P(SEQ, None),
        P(SEQ, DP),
        P(None, SEQ, DP),
        P(None, SEQ, DP),
    )
    out_specs = (P(SEQ, DP), P(None, SEQ, DP), P(None, SEQ, DP))
    return jax.shard_map(local, mesh=fine, in_specs=in_specs, out_specs=out_specs, check_vma=False)
```

```python
import math

import jax
import jax.numpy as jnp
from jax import lax
from jax.experimental import pallas as pl
from jax.experimental.pallas import tpu as pltpu
from jax.sharding import Mesh, PartitionSpec as P

KWIDTH = 5
HALF = 2
DP = ("x", "zl")
SEQ = ("zh", "y", "c")
NZ, NY, NC = 4, 4, 2
BF = jnp.bfloat16
F32 = jnp.float32
PARAMS = pltpu.CompilerParams(vmem_limit_bytes=40 * 1024 * 1024)
VMEM = pl.BlockSpec(memory_space=pltpu.VMEM)
SMEM = pl.BlockSpec(memory_space=pltpu.SMEM)
HBM = pl.BlockSpec(memory_space=pltpu.HBM)


def half_slope(pre_act):
    values = pre_act.astype(F32)
    cumulative = 0.5 * (1.0 + lax.erf(values * (1.0 / math.sqrt(2.0))))
    density = jnp.exp(-0.5 * values * values) * (1.0 / math.sqrt(2.0 * math.pi))
    return 0.5 * (cumulative + values * density)


def shifted(block, axis, count, step):
    return lax.ppermute(block, axis, [(i, (i + step) % count) for i in range(count)])


def scatter_rows(keep, send):
    total = keep + shifted(send, "c", NC, 1).astype(F32)
    parts = [shifted(total[s].astype(BF), "y", NY, s) for s in range(1, NY)]
    total = total[0] + sum(p.astype(F32) for p in parts)
    parts = [shifted(total[s].astype(BF), "zh", NZ, s) for s in range(1, NZ)]
    return total[0] + sum(p.astype(F32) for p in parts)


def doubling():
    row = lax.broadcasted_iota(jnp.int32, (128, 256), 0)
    col = lax.broadcasted_iota(jnp.int32, (128, 256), 1)
    return (row == lax.shift_right_logical(col, 1)).astype(F32).astype(BF)


def mm(a, b):
    return jnp.dot(a, b, preferred_element_type=F32)


def one_hot(rows, start, pads):
    row = lax.broadcasted_iota(jnp.int32, (rows, 512), 0)
    col = lax.broadcasted_iota(jnp.int32, (rows, 512), 1)
    place = row + start
    if pads:
        for edge in (22, 44, 66):
            place = place + jnp.where(row >= edge, 2, 0)
    return (place == col).astype(F32).astype(BF)


def pack_kernel(tower_ref, upper_ref, lower_ref, out_ref, weight_ref, tower_rows_ref, buf_ref, sem):
    weight_ref[...] = jnp.zeros((48, 512), F32)
    weight_ref[0:22, :] = sum(mm(upper_ref[k], one_hot(96, 96 * k, False)) for k in range(KWIDTH))
    weight_ref[24:44, :] = sum(mm(lower_ref[k], one_hot(88, 96 * k, True)) for k in range(KWIDTH))
    weight = weight_ref[...].astype(BF)
    tower = tower_ref[...].astype(F32)
    tower_rows_ref[...] = jnp.zeros((128, 512), F32)
    for p in range(16):
        at, row = 512 * p, 8 * p
        tower_rows_ref[row : row + 3, :] = tower[:, at : at + 512]
        if p > 0:
            tower_rows_ref[row + 3 : row + 6, 0:128] = tower[:, at - 128 : at]
        tower_rows_ref[row + 3 : row + 6, 128:256] = tower[:, at + 256 : at + 384]
        tower_rows_ref[row + 3 : row + 6, 256:384] = tower[:, at + 128 : at + 256]
        if p < 15:
            tower_rows_ref[row + 3 : row + 6, 384:512] = tower[:, at + 512 : at + 640]
        buf_ref[p, 0:48, :] = weight
        buf_ref[p, 48:56, :] = tower_rows_ref[row : row + 8, :].astype(BF)
        pltpu.make_async_copy(buf_ref.at[p], out_ref.at[p], sem.at[p]).start()
    for p in range(16):
        pltpu.make_async_copy(buf_ref.at[p], out_ref.at[p], sem.at[p]).wait()


def upper_kernel(
    pos_ref, slope_ref, own_ref, other_ref, mid_ref, taps_ref, main_ref, edge_ref, w_ref, halo_ref, buf_ref, sem
):
    first = pos_ref[2] == 0
    for p in range(16):
        own, other = own_ref[p, 48:56, :].astype(F32), other_ref[p, 48:56, :].astype(F32)
        for j in range(2):
            rows = jnp.where(first, own, other) if j == 0 else jnp.where(first, other, own)
            rows = jnp.where(first, rows[:, 0:256], rows[:, 256:512])
            at = 3 * (2 * p + j)
            main_ref[at : at + 3, :] = rows[0:3]
            edge_ref[at : at + 3, :] = rows[3:6]
        own, other = own_ref[p, 0:24, :].astype(F32), other_ref[p, 0:24, :].astype(F32)
        both = [jnp.where(first, own, other), jnp.where(first, other, own)]
        w_ref[48 * p : 48 * p + 48, :] = jnp.concatenate(both, axis=0).astype(BF)
    spread = doubling()
    main = main_ref[...].astype(BF)
    edge = edge_ref[...].astype(BF)
    grad = jnp.concatenate(
        [
            mm(edge[:, :128], spread)[:, 128:],
            mm(main[:, :128], spread),
            mm(main[:, 128:], spread),
            mm(edge[:, 128:], spread)[:, :128],
        ],
        axis=1,
    )
    grad = grad * slope_ref[...]
    lane = lax.broadcasted_iota(jnp.int32, (96, 128), 1)
    taps_ref[480:512, :] = jnp.zeros((32, 512), BF)
    halo_ref[480:512, :] = jnp.zeros((32, 128), F32)
    for k in range(KWIDTH):
        moved = pltpu.roll(grad, 768 - (130 - k), 1)
        after = pltpu.roll(moved[:, 512:640], 126, 1)
        taps_ref[96 * k : 96 * k + 96, :] = moved[:, 0:512].astype(BF)
        halo_ref[96 * k : 96 * k + 96, :] = jnp.where(lane == 127, moved[:, 640:768], after)
    outside = lax.dot_general(
        halo_ref[...].T.astype(BF), w_ref[...], (((1,), (1,)), ((), ())), preferred_element_type=F32
    )[120:128]
    row = lax.broadcasted_iota(jnp.int32, (8, 512), 0)
    taps = taps_ref[...]
    for d in range(8):
        mid = mm(w_ref[96 * d : 96 * d + 96, :], taps)
        moved = pltpu.roll(outside, (768 - 96 * d) % 768, 1)[:, 0:512]
        buf_ref[d] = jnp.concatenate([mid[0:16], jnp.where(row >= 6, moved, mid[16:24]), mid[24:]], axis=0).astype(BF)
        pltpu.make_async_copy(buf_ref.at[d], mid_ref.at[d], sem.at[d]).start()
    for d in range(8):
        pltpu.make_async_copy(buf_ref.at[d], mid_ref.at[d], sem.at[d]).wait()


def lower_weight_kernel(pos_ref, own_ref, other_ref, out_ref, rows_ref):
    first = pos_ref[2] == 0
    for p in range(16):
        own, other = own_ref[p, 24:48, :].astype(F32), other_ref[p, 24:48, :].astype(F32)
        rows_ref[40 * p : 40 * p + 24, :] = jnp.where(first, own, other)
        rows_ref[40 * p + 20 : 40 * p + 44, :] = jnp.where(first, other, own)
    out_ref[...] = rows_ref[0:640, :].astype(BF)


def lower_kernel(pos_ref, mid_ref, slope_ref, w_ref, low_ref, taps_ref, buf_ref, sem):
    place = pos_ref[0] * (NY * NC) + pos_ref[1] * NC + pos_ref[2]
    total = mid_ref[0].astype(F32)
    for d in range(1, 8):
        total = total + mid_ref[d].astype(F32)
    mid = total.astype(BF)
    ends = mid[:, 0:128].astype(F32).T
    left = jnp.broadcast_to(jnp.where(place == 0, 0.0, ends[0:96, 23:24]), (96, 128))
    right = jnp.broadcast_to(jnp.where(place == 31, 0.0, ends[0:96, 22:23]), (96, 128))
    spread = doubling()
    grad = jnp.concatenate(
        [left] + [mm(mid[:, 128 * j : 128 * j + 128], spread) for j in range(4)] + [right], axis=1
    )
    grad = grad * slope_ref[...]
    taps_ref[480:512, :] = jnp.zeros((32, 1024), BF)
    for k in range(KWIDTH):
        moved = pltpu.roll(grad, 1280 - (130 - k), 1)
        taps_ref[96 * k : 96 * k + 96, :] = moved[:, 0:1024].astype(BF)
    taps = taps_ref[...]
    for d in range(8):
        buf_ref[d] = mm(w_ref[80 * d : 80 * d + 80, :], taps).astype(BF)
        pltpu.make_async_copy(buf_ref.at[d], low_ref.at[d], sem.at[d]).start()
    for d in range(8):
        pltpu.make_async_copy(buf_ref.at[d], low_ref.at[d], sem.at[d]).wait()


def total_kernel(low_ref, out_ref):
    total = low_ref[0].astype(F32)
    for d in range(1, 8):
        total = total + low_ref[d].astype(F32)
    out_ref[...] = total.astype(BF)


def weight_grad_kernel(pos_ref, act_ref, taps_ref, keep_ref, send_ref, rows_ref, block_ref):
    channels, count = act_ref.shape
    width = channels // 32
    rows_ref[channels:, :] = jnp.zeros((8, rows_ref.shape[1]), F32)
    rows_ref[0:channels, :] = lax.dot_general(
        act_ref[...], taps_ref[:, 0:count], (((1,), (1,)), ((), ())), preferred_element_type=F32
    )
    for q in range(32):
        block_ref[q] = rows_ref[width * q : width * q + 24, :]
    for ry in range(NY):
        for rz in range(NZ):
            zh = lax.rem(pos_ref[0] + rz, NZ)
            y = lax.rem(pos_ref[1] + ry, NY)
            base = (zh * NY + y) * NC
            keep_ref[ry, rz] = block_ref[base + pos_ref[2]]
            send_ref[ry, rz] = block_ref[base + 1 - pos_ref[2]].astype(BF)


def weight_grad(pos, act, taps):
    block = (NY, NZ, 24, taps.shape[0])
    return pl.pallas_call(
        weight_grad_kernel,
        out_shape=(jax.ShapeDtypeStruct(block, F32), jax.ShapeDtypeStruct(block, BF)),
        in_specs=[SMEM, VMEM, VMEM],
        out_specs=(VMEM, VMEM),
        scratch_shapes=[pltpu.VMEM((act.shape[0] + 8, taps.shape[0]), F32), pltpu.VMEM((32, 24, taps.shape[0]), F32)],
        compiler_params=PARAMS,
        name="weight_grad",
    )(pos, act, taps)


def neighbours(block):
    count = NZ * NY * NC
    forward = [(i, i + 1) for i in range(count - 1)]
    backward = [(i + 1, i) for i in range(count - 1)]
    low = lax.ppermute(block[:, :, -128:], SEQ, forward)
    high = lax.ppermute(block[:, :, :128], SEQ, backward)
    return low, high


def local(tower_grad, act_mid, pre_mid, act_low, pre_low, weight_upper, weight_lower):
    pos = jnp.stack([lax.axis_index("zh"), lax.axis_index("y"), lax.axis_index("c")]).astype(jnp.int32)
    packed = pl.pallas_call(
        pack_kernel,
        out_shape=jax.ShapeDtypeStruct((16, 56, 512), BF),
        in_specs=[VMEM] * 3,
        out_specs=HBM,
        scratch_shapes=[
            pltpu.VMEM((48, 512), F32),
            pltpu.VMEM((128, 512), F32),
            pltpu.VMEM((16, 56, 512), BF),
            pltpu.SemaphoreType.DMA((16,)),
        ],
        compiler_params=PARAMS,
        name="pack",
    )(tower_grad.T, weight_upper, weight_lower)
    own = lax.all_to_all(packed, ("zh", "y"), split_axis=0, concat_axis=0, tiled=True)
    other = shifted(own, "c", NC, 1)

    pre_upper = pre_mid.T
    pre_lower = jnp.pad(pre_low.T.reshape(4, 22, 1024), ((0, 0), (0, 2), (0, 0))).reshape(96, 1024)
    edges = jnp.stack(
        [
            jnp.concatenate([pre_upper[:, :128], pre_upper[:, -128:]], axis=1),
            jnp.concatenate([pre_lower[:, :128], pre_lower[:, -128:]], axis=1),
        ]
    )
    low_side, high_side = neighbours(edges)
    slope_upper = half_slope(jnp.concatenate([low_side[0], pre_upper, high_side[0]], axis=1))
    slope_lower = half_slope(jnp.concatenate([low_side[1], pre_lower, high_side[1]], axis=1))

    mid_part, upper_taps = pl.pallas_call(
        upper_kernel,
        out_shape=(jax.ShapeDtypeStruct((8, 96, 512), BF), jax.ShapeDtypeStruct((512, 512), BF)),
        in_specs=[SMEM] + [VMEM] * 3,
        out_specs=(HBM, VMEM),
        scratch_shapes=[
            pltpu.VMEM((96, 256), F32),
            pltpu.VMEM((96, 256), F32),
            pltpu.VMEM((768, 512), BF),
            pltpu.VMEM((512, 128), F32),
            pltpu.VMEM((8, 96, 512), BF),
            pltpu.SemaphoreType.DMA((8,)),
        ],
        compiler_params=PARAMS,
        name="upper",
    )(pos, slope_upper, own, other)
    mid_parts = lax.all_to_all(mid_part, DP, split_axis=0, concat_axis=0, tiled=True)

    upper_sum = scatter_rows(*weight_grad(pos, act_mid.T, upper_taps))
    lower_full = pl.pallas_call(
        lower_weight_kernel,
        out_shape=jax.ShapeDtypeStruct((640, 512), BF),
        in_specs=[SMEM] + [VMEM] * 2,
        out_specs=VMEM,
        scratch_shapes=[pltpu.VMEM((648, 512), F32)],
        compiler_params=PARAMS,
        name="lower_weight",
    )(pos, own, other)

    low_part, lower_taps = pl.pallas_call(
        lower_kernel,
        out_shape=(jax.ShapeDtypeStruct((8, 80, 1024), BF), jax.ShapeDtypeStruct((512, 1024), BF)),
        in_specs=[SMEM] + [VMEM] * 3,
        out_specs=(HBM, VMEM),
        scratch_shapes=[pltpu.VMEM((8, 80, 1024), BF), pltpu.SemaphoreType.DMA((8,))],
        compiler_params=PARAMS,
        name="lower",
    )(pos, mid_parts, slope_lower, lower_full)
    low_parts = lax.all_to_all(low_part, DP, split_axis=0, concat_axis=0, tiled=True)
    lower_sum = scatter_rows(*weight_grad(pos, act_low.T, lower_taps))

    low_grad = pl.pallas_call(
        total_kernel,
        out_shape=jax.ShapeDtypeStruct((80, 1024), BF),
        in_specs=[VMEM],
        out_specs=VMEM,
        compiler_params=PARAMS,
        name="low_total",
    )(low_parts).T
    mid_total = act_mid.shape[0] * NZ * NY * NC
    low_total = act_low.shape[0] * NZ * NY * NC
    grad_upper = upper_sum[:22, :480].reshape(22, 5, 96).transpose(1, 0, 2) * (1.0 / math.sqrt(mid_total))
    grad_lower = lower_sum[:20, :480].reshape(20, 5, 4, 24)[:, :, :, :22].reshape(20, 5, 88)
    grad_lower = grad_lower.transpose(1, 0, 2) * (1.0 / math.sqrt(low_total))
    return low_grad, grad_upper, grad_lower


def solution(mesh):
    fine = Mesh(mesh.devices.reshape(4, 2, NZ, NY, NC), DP + SEQ)
    in_specs = (
        P(None, DP + SEQ),
        P(SEQ, None),
        P(SEQ, DP),
        P(SEQ, None),
        P(SEQ, DP),
        P(None, SEQ, DP),
        P(None, SEQ, DP),
    )
    out_specs = (P(SEQ, DP), P(None, SEQ, DP), P(None, SEQ, DP))
    return jax.shard_map(local, mesh=fine, in_specs=in_specs, out_specs=out_specs, check_vma=False)
```

```python
import functools
import math

import jax
import jax.numpy as jnp
from jax import lax
from jax.experimental import pallas as pl
from jax.experimental.pallas import tpu as pltpu
from jax.sharding import Mesh, PartitionSpec as P

KWIDTH = 5
HALF = 2
DP = ("x", "zl")
SEQ = ("zh", "y", "c")
NZ, NY, NC = 4, 4, 2
BF = jnp.bfloat16
F32 = jnp.float32
PARAMS = pltpu.CompilerParams(vmem_limit_bytes=16 * 1024 * 1024)
VMEM = pl.BlockSpec(memory_space=pltpu.VMEM)
SMEM = pl.BlockSpec(memory_space=pltpu.SMEM)
HBM = pl.BlockSpec(memory_space=pltpu.HBM)


def half_slope(pre_act):
    values = pre_act.astype(F32)
    cumulative = 0.5 * (1.0 + lax.erf(values * (1.0 / math.sqrt(2.0))))
    density = jnp.exp(-0.5 * values * values) * (1.0 / math.sqrt(2.0 * math.pi))
    return 0.5 * (cumulative + values * density)


def shifted(block, axis, count, step):
    return lax.ppermute(block, axis, [(i, (i + step) % count) for i in range(count)])


def join_kernel(*refs):
    out_ref = refs[-1]
    for s in range(NY):
        out_ref[NZ * s : NZ * s + NZ] = refs[s][...]


def join(levels):
    shape = (NY * NZ,) + levels[0].shape[1:]
    return pl.pallas_call(
        join_kernel,
        out_shape=jax.ShapeDtypeStruct(shape, BF),
        in_specs=[VMEM] * NY,
        out_specs=VMEM,
        compiler_params=PARAMS,
        name="join",
    )(*levels)


def core_sum_kernel(keep_upper_ref, got_upper_ref, keep_lower_ref, got_lower_ref, own_ref, *send_refs):
    pairs = ((keep_upper_ref, got_upper_ref), (keep_lower_ref, got_lower_ref))
    for half, (keep_ref, got_ref) in enumerate(pairs):
        rows = slice(24 * half, 24 * half + 24)
        for s in range(NY):
            for z in range(NZ):
                total = keep_ref[s, z] + got_ref[s, z].astype(F32)
                if s == 0:
                    own_ref[z, rows] = total
                else:
                    send_refs[s - 1][z, rows] = total.astype(BF)


def y_sum_kernel(own_ref, *refs):
    got_refs, total_ref, send_refs = refs[: NY - 1], refs[NY - 1], refs[NY:]
    for z in range(NZ):
        total = own_ref[z]
        for got_ref in got_refs:
            total = total + got_ref[z].astype(F32)
        if z == 0:
            total_ref[...] = total
        else:
            send_refs[z - 1][...] = total.astype(BF)


def z_sum_kernel(scales, own_ref, *refs):
    got_refs, upper_ref, lower_ref = refs[: NZ - 1], refs[NZ - 1], refs[NZ]
    total = own_ref[...]
    for got_ref in got_refs:
        total = total + got_ref[...].astype(F32)
    lane = lax.broadcasted_iota(jnp.int32, (24, 512), 1)
    for k in range(KWIDTH):
        upper_ref[k] = pltpu.roll(total[0:24], (512 - 96 * k) % 512, 1)[0:22, 0:96] * scales[0]
        lower = pltpu.roll(total[24:48], (512 - 96 * k) % 512, 1)
        packed = lower
        for group in range(1, 4):
            packed = jnp.where(lane >= 22 * group, pltpu.roll(lower, 512 - 2 * group, 1), packed)
        lower_ref[k] = packed[0:20, 0:88] * scales[1]


def small_call(kernel, name, out_shape, *operands):
    return pl.pallas_call(
        kernel,
        out_shape=out_shape,
        in_specs=[VMEM] * len(operands),
        out_specs=tuple(VMEM for _ in out_shape),
        compiler_params=PARAMS,
        name=name,
    )(*operands)


def core_sum(upper, lower):
    level = jax.ShapeDtypeStruct((NZ, 48, 512), BF)
    outs = (jax.ShapeDtypeStruct(level.shape, F32),) + (level,) * (NY - 1)
    return small_call(core_sum_kernel, "core_sum", outs, *upper, *lower)


def z_sum(own, got, scales, upper_shape, lower_shape):
    block = jax.ShapeDtypeStruct((48, 512), BF)
    own, *sends = small_call(
        y_sum_kernel, "y_sum", (jax.ShapeDtypeStruct(block.shape, F32),) + (block,) * (NZ - 1), own, *got
    )
    got = [shifted(send, "zh", NZ, s + 1) for s, send in enumerate(sends)]
    outs = (jax.ShapeDtypeStruct(upper_shape, F32), jax.ShapeDtypeStruct(lower_shape, F32))
    return small_call(functools.partial(z_sum_kernel, scales), "z_sum", outs, own, *got)


def doubling():
    row = lax.broadcasted_iota(jnp.int32, (128, 256), 0)
    col = lax.broadcasted_iota(jnp.int32, (128, 256), 1)
    return (row == lax.shift_right_logical(col, 1)).astype(F32).astype(BF)


def mm(a, b):
    return jnp.dot(a, b, preferred_element_type=F32)


def one_hot(rows, start, pads):
    row = lax.broadcasted_iota(jnp.int32, (rows, 512), 0)
    col = lax.broadcasted_iota(jnp.int32, (rows, 512), 1)
    place = row + start
    if pads:
        for edge in (22, 44, 66):
            place = place + jnp.where(row >= edge, 2, 0)
    return (place == col).astype(F32).astype(BF)


def pack_kernel(
    tower_hbm, upper_hbm, lower_hbm, out_ref, lower_out_ref,
    tower_ref, upper_ref, lower_ref, weight_ref, tower_rows_ref, buf_ref, sem, in_sem,
):
    copies = [
        pltpu.make_async_copy(source, target, in_sem.at[i])
        for i, (source, target) in enumerate(((upper_hbm, upper_ref), (lower_hbm, lower_ref), (tower_hbm, tower_ref)))
    ]
    for copy in copies:
        copy.start()
    for copy in copies:
        copy.wait()
    weight_ref[...] = jnp.zeros((48, 512), F32)
    weight_ref[0:22, :] = sum(mm(upper_ref[k], one_hot(96, 96 * k, False)) for k in range(KWIDTH))
    weight_ref[24:44, :] = sum(mm(lower_ref[k], one_hot(88, 96 * k, True)) for k in range(KWIDTH))
    weight = weight_ref[0:24, :].astype(BF)
    lower_out_ref[...] = weight_ref[24:48, :].astype(BF)
    tower = tower_ref[...].astype(F32)
    tower_rows_ref[...] = jnp.zeros((128, 512), F32)
    for p in range(16):
        at, row = 512 * p, 8 * p
        tower_rows_ref[row : row + 3, :] = tower[:, at : at + 512]
        if p > 0:
            tower_rows_ref[row + 3 : row + 6, 0:128] = tower[:, at - 128 : at]
        tower_rows_ref[row + 3 : row + 6, 128:256] = tower[:, at + 256 : at + 384]
        tower_rows_ref[row + 3 : row + 6, 256:384] = tower[:, at + 128 : at + 256]
        if p < 15:
            tower_rows_ref[row + 3 : row + 6, 384:512] = tower[:, at + 512 : at + 640]
        buf_ref[p, 0:24, :] = weight
        buf_ref[p, 24:32, :] = tower_rows_ref[row : row + 8, :].astype(BF)
        pltpu.make_async_copy(buf_ref.at[p], out_ref.at[p], sem.at[p]).start()
    for p in range(16):
        pltpu.make_async_copy(buf_ref.at[p], out_ref.at[p], sem.at[p]).wait()


def upper_kernel(
    pos_ref, slope_ref, own_ref, other_ref, mid_ref, taps_ref, main_ref, edge_ref, w_ref, halo_ref, buf_ref, sem
):
    first = pos_ref[2] == 0
    for p in range(16):
        own, other = own_ref[p, 24:32, :].astype(F32), other_ref[p, 24:32, :].astype(F32)
        for j in range(2):
            rows = jnp.where(first, own, other) if j == 0 else jnp.where(first, other, own)
            rows = jnp.where(first, rows[:, 0:256], rows[:, 256:512])
            at = 3 * (2 * p + j)
            main_ref[at : at + 3, :] = rows[0:3]
            edge_ref[at : at + 3, :] = rows[3:6]
        own, other = own_ref[p, 0:24, :].astype(F32), other_ref[p, 0:24, :].astype(F32)
        both = [jnp.where(first, own, other), jnp.where(first, other, own)]
        w_ref[48 * p : 48 * p + 48, :] = jnp.concatenate(both, axis=0).astype(BF)
    spread = doubling()
    main = main_ref[...].astype(BF)
    edge = edge_ref[...].astype(BF)
    grad = jnp.concatenate(
        [
            mm(edge[:, :128], spread)[:, 128:],
            mm(main[:, :128], spread),
            mm(main[:, 128:], spread),
            mm(edge[:, 128:], spread)[:, :128],
        ],
        axis=1,
    )
    grad = grad * slope_ref[...]
    lane = lax.broadcasted_iota(jnp.int32, (96, 128), 1)
    taps_ref[480:512, :] = jnp.zeros((32, 512), BF)
    halo_ref[480:512, :] = jnp.zeros((32, 128), F32)
    for k in range(KWIDTH):
        moved = pltpu.roll(grad, 768 - (130 - k), 1)
        after = pltpu.roll(moved[:, 512:640], 126, 1)
        taps_ref[96 * k : 96 * k + 96, :] = moved[:, 0:512].astype(BF)
        halo_ref[96 * k : 96 * k + 96, :] = jnp.where(lane == 127, moved[:, 640:768], after)
    outside = lax.dot_general(
        halo_ref[...].T.astype(BF), w_ref[...], (((1,), (1,)), ((), ())), preferred_element_type=F32
    )[120:128]
    row = lax.broadcasted_iota(jnp.int32, (8, 256), 0)
    for half in range(2):
        lanes = slice(256 * half, 256 * half + 256)
        mid = mm(w_ref[...], taps_ref[:, lanes])
        for d in range(8):
            part = mid[96 * d : 96 * d + 96]
            if half == 0:
                moved = pltpu.roll(outside, (768 - 96 * d) % 768, 1)[:, 0:256]
                part = jnp.concatenate([part[0:16], jnp.where(row >= 6, moved, part[16:24]), part[24:]], axis=0)
            buf_ref[d, :, lanes] = part.astype(BF)
    for d in range(8):
        pltpu.make_async_copy(buf_ref.at[d], mid_ref.at[d], sem.at[d]).start()
    for d in range(8):
        pltpu.make_async_copy(buf_ref.at[d], mid_ref.at[d], sem.at[d]).wait()


def lower_weight_kernel(pos_ref, own_ref, other_ref, out_ref, rows_ref):
    first = pos_ref[2] == 0
    for p in range(16):
        slot = lax.rem(pos_ref[1] - p % NY + NY, NY) * NZ + lax.rem(pos_ref[0] - p // NY + NZ, NZ)
        own, other = own_ref[slot].astype(F32), other_ref[slot].astype(F32)
        rows_ref[40 * p : 40 * p + 24, :] = jnp.where(first, own, other)
        rows_ref[40 * p + 20 : 40 * p + 44, :] = jnp.where(first, other, own)
    out_ref[...] = rows_ref[0:640, :].astype(BF)


def lower_kernel(pos_ref, mid_ref, slope_ref, w_ref, low_ref, taps_ref, buf_ref, sem):
    place = pos_ref[0] * (NY * NC) + pos_ref[1] * NC + pos_ref[2]
    total = mid_ref[0].astype(F32)
    for d in range(1, 8):
        total = total + mid_ref[d].astype(F32)
    mid = total.astype(BF)
    ends = mid[:, 0:128].astype(F32).T
    left = jnp.broadcast_to(jnp.where(place == 0, 0.0, ends[0:96, 23:24]), (96, 128))
    right = jnp.broadcast_to(jnp.where(place == 31, 0.0, ends[0:96, 22:23]), (96, 128))
    spread = doubling()
    grad = jnp.concatenate(
        [left] + [mm(mid[:, 128 * j : 128 * j + 128], spread) for j in range(4)] + [right], axis=1
    )
    grad = grad * slope_ref[...]
    taps_ref[480:512, :] = jnp.zeros((32, 1024), BF)
    for k in range(KWIDTH):
        moved = pltpu.roll(grad, 1280 - (130 - k), 1)
        taps_ref[96 * k : 96 * k + 96, :] = moved[:, 0:1024].astype(BF)
    for quarter in range(4):
        lanes = slice(256 * quarter, 256 * quarter + 256)
        low = mm(w_ref[...], taps_ref[:, lanes])
        for d in range(8):
            buf_ref[d, :, lanes] = low[80 * d : 80 * d + 80].astype(BF)
        pltpu.make_async_copy(buf_ref.at[:, :, lanes], low_ref.at[:, :, lanes], sem.at[quarter]).start()
    for quarter in range(4):
        lanes = slice(256 * quarter, 256 * quarter + 256)
        pltpu.make_async_copy(buf_ref.at[:, :, lanes], low_ref.at[:, :, lanes], sem.at[quarter]).wait()


def total_kernel(low_ref, out_ref):
    total = low_ref[0].astype(F32)
    for d in range(1, 8):
        total = total + low_ref[d].astype(F32)
    out_ref[...] = total.astype(BF)


def weight_grad_kernel(pos_ref, act_ref, taps_ref, keep_ref, send_ref, rows_ref, block_ref):
    channels, count = act_ref.shape
    width = channels // 32
    rows_ref[channels:, :] = jnp.zeros((8, rows_ref.shape[1]), F32)
    rows_ref[0:channels, :] = lax.dot_general(
        act_ref[...], taps_ref[:, 0:count], (((1,), (1,)), ((), ())), preferred_element_type=F32
    )
    for q in range(32):
        block_ref[q] = rows_ref[width * q : width * q + 24, :]
    for ry in range(NY):
        for rz in range(NZ):
            zh = lax.rem(pos_ref[0] + rz, NZ)
            y = lax.rem(pos_ref[1] + ry, NY)
            base = (zh * NY + y) * NC
            keep_ref[ry, rz] = block_ref[base + pos_ref[2]]
            send_ref[ry, rz] = block_ref[base + 1 - pos_ref[2]].astype(BF)


def weight_grad(pos, act, taps):
    block = (NY, NZ, 24, taps.shape[0])
    return pl.pallas_call(
        weight_grad_kernel,
        out_shape=(jax.ShapeDtypeStruct(block, F32), jax.ShapeDtypeStruct(block, BF)),
        in_specs=[SMEM, VMEM, VMEM],
        out_specs=(VMEM, VMEM),
        scratch_shapes=[pltpu.VMEM((act.shape[0] + 8, taps.shape[0]), F32), pltpu.VMEM((32, 24, taps.shape[0]), F32)],
        compiler_params=PARAMS,
        name="weight_grad",
    )(pos, act, taps)


def neighbours(block):
    count = NZ * NY * NC
    forward = [(i, i + 1) for i in range(count - 1)]
    backward = [(i + 1, i) for i in range(count - 1)]
    low = lax.ppermute(block[:, :, -128:], SEQ, forward)
    high = lax.ppermute(block[:, :, :128], SEQ, backward)
    return low, high


def local(tower_grad, act_mid, pre_mid, act_low, pre_low, weight_upper, weight_lower):
    pos = jnp.stack([lax.axis_index("zh"), lax.axis_index("y"), lax.axis_index("c")]).astype(jnp.int32)
    packed, lower_block = pl.pallas_call(
        pack_kernel,
        out_shape=(jax.ShapeDtypeStruct((16, 32, 512), BF), jax.ShapeDtypeStruct((24, 512), BF)),
        in_specs=[HBM] * 3,
        out_specs=(HBM, VMEM),
        scratch_shapes=[
            pltpu.VMEM((3, 8192), BF),
            pltpu.VMEM(weight_upper.shape, BF),
            pltpu.VMEM(weight_lower.shape, BF),
            pltpu.VMEM((48, 512), F32),
            pltpu.VMEM((128, 512), F32),
            pltpu.VMEM((16, 32, 512), BF),
            pltpu.SemaphoreType.DMA((16,)),
            pltpu.SemaphoreType.DMA((3,)),
        ],
        compiler_params=PARAMS,
        name="pack",
    )(*(pltpu.with_memory_space_constraint(v, pltpu.HBM) for v in (tower_grad.T, weight_upper, weight_lower)))
    pre_upper = pre_mid.T
    pre_lower = jnp.pad(pre_low.T.reshape(4, 22, 1024), ((0, 0), (0, 2), (0, 0))).reshape(96, 1024)
    edges = jnp.stack(
        [
            jnp.concatenate([pre_upper[:, :128], pre_upper[:, -128:]], axis=1),
            jnp.concatenate([pre_lower[:, :128], pre_lower[:, -128:]], axis=1),
        ]
    )
    low_side, high_side = neighbours(edges)
    lower_level = jnp.stack([lower_block] + [shifted(lower_block, "zh", NZ, s) for s in range(1, NZ)])
    own = lax.all_to_all(packed, ("zh", "y"), split_axis=0, concat_axis=0, tiled=True)
    own, low_side, high_side, lower_level = lax.optimization_barrier((own, low_side, high_side, lower_level))
    other = shifted(own, "c", NC, 1)
    slope_upper = half_slope(jnp.concatenate([low_side[0], pre_upper, high_side[0]], axis=1))
    slope_lower = half_slope(jnp.concatenate([low_side[1], pre_lower, high_side[1]], axis=1))

    mid_part, upper_taps = pl.pallas_call(
        upper_kernel,
        out_shape=(jax.ShapeDtypeStruct((8, 96, 512), BF), jax.ShapeDtypeStruct((512, 512), BF)),
        in_specs=[SMEM] + [VMEM] * 3,
        out_specs=(HBM, VMEM),
        scratch_shapes=[
            pltpu.VMEM((96, 256), F32),
            pltpu.VMEM((96, 256), F32),
            pltpu.VMEM((768, 512), BF),
            pltpu.VMEM((512, 128), F32),
            pltpu.VMEM((8, 96, 512), BF),
            pltpu.SemaphoreType.DMA((8,)),
        ],
        compiler_params=PARAMS,
        name="upper",
    )(pos, slope_upper, own, other)
    mid_parts = lax.all_to_all(mid_part, DP, split_axis=0, concat_axis=0, tiled=True)

    lower_levels = [lower_level] + [shifted(lower_level, "y", NY, s) for s in range(1, NY)]
    upper_keep, upper_send = weight_grad(pos, act_mid.T, upper_taps)
    upper_got = shifted(upper_send, "c", NC, 1)
    lower_levels, upper_send = lax.optimization_barrier((lower_levels, upper_send))
    lower_own = join(lower_levels)
    lower_other = shifted(lower_own, "c", NC, 1)
    lower_full = pl.pallas_call(
        lower_weight_kernel,
        out_shape=jax.ShapeDtypeStruct((640, 512), BF),
        in_specs=[SMEM] + [VMEM] * 2,
        out_specs=VMEM,
        scratch_shapes=[pltpu.VMEM((648, 512), F32)],
        compiler_params=PARAMS,
        name="lower_weight",
    )(pos, lower_own, lower_other)

    lower_full, act_low = lax.optimization_barrier((lower_full, act_low))
    act_low_rows = act_low.T
    mid_parts, upper_got, act_low_rows = lax.optimization_barrier((mid_parts, upper_got, act_low_rows))
    low_part, lower_taps = pl.pallas_call(
        lower_kernel,
        out_shape=(jax.ShapeDtypeStruct((8, 80, 1024), BF), jax.ShapeDtypeStruct((512, 1024), BF)),
        in_specs=[SMEM] + [VMEM] * 3,
        out_specs=(HBM, VMEM),
        scratch_shapes=[pltpu.VMEM((8, 80, 1024), BF), pltpu.SemaphoreType.DMA((4,))],
        compiler_params=PARAMS,
        name="lower",
    )(pos, mid_parts, slope_lower, lower_full)
    lower_keep, lower_send = weight_grad(pos, act_low_rows, lower_taps)
    low_part, _ = lax.optimization_barrier((low_part, lower_keep))
    lower_got = shifted(lower_send, "c", NC, 1)
    own_sum, *sends = core_sum((upper_keep, upper_got), (lower_keep, lower_got))
    got = [shifted(send, "y", NY, s + 1) for s, send in enumerate(sends)]
    low_parts = lax.all_to_all(low_part, DP, split_axis=0, concat_axis=0, tiled=True)
    scales = tuple(1.0 / math.sqrt(act.shape[0] * NZ * NY * NC) for act in (act_mid, act_low))
    grad_upper, grad_lower = z_sum(own_sum, got, scales, weight_upper.shape, weight_lower.shape)

    low_grad = pl.pallas_call(
        total_kernel,
        out_shape=jax.ShapeDtypeStruct((80, 1024), BF),
        in_specs=[VMEM],
        out_specs=VMEM,
        compiler_params=PARAMS,
        name="low_total",
    )(low_parts).T
    return low_grad, grad_upper, grad_lower


def solution(mesh):
    fine = Mesh(mesh.devices.reshape(4, 2, NZ, NY, NC), DP + SEQ)
    in_specs = (
        P(None, DP + SEQ),
        P(SEQ, None),
        P(SEQ, DP),
        P(SEQ, None),
        P(SEQ, DP),
        P(None, SEQ, DP),
        P(None, SEQ, DP),
    )
    out_specs = (P(SEQ, DP), P(None, SEQ, DP), P(None, SEQ, DP))
    return jax.shard_map(local, mesh=fine, in_specs=in_specs, out_specs=out_specs, check_vma=False)
```

```python
import functools
import math

import jax
import jax.numpy as jnp
from jax import lax
from jax.experimental import pallas as pl
from jax.experimental.pallas import tpu as pltpu
from jax.sharding import Mesh, PartitionSpec as P

KWIDTH = 5
HALF = 2
DP = ("x", "zl")
SEQ = ("zh", "y", "c")
NZ, NY, NC = 4, 4, 2
BF = jnp.bfloat16
F32 = jnp.float32
PARAMS = pltpu.CompilerParams(vmem_limit_bytes=16 * 1024 * 1024)
VMEM = pl.BlockSpec(memory_space=pltpu.VMEM)
SMEM = pl.BlockSpec(memory_space=pltpu.SMEM)
HBM = pl.BlockSpec(memory_space=pltpu.HBM)


def half_slope(pre_act):
    values = pre_act.astype(F32)
    cumulative = 0.5 * (1.0 + lax.erf(values * (1.0 / math.sqrt(2.0))))
    density = jnp.exp(-0.5 * values * values) * (1.0 / math.sqrt(2.0 * math.pi))
    return 0.5 * (cumulative + values * density)


def shifted(block, axis, count, step):
    return lax.ppermute(block, axis, [(i, (i + step) % count) for i in range(count)])


def join_kernel(*refs):
    out_ref = refs[-1]
    for s in range(NY):
        out_ref[NZ * s : NZ * s + NZ] = refs[s][...]


def join(levels):
    shape = (NY * NZ,) + levels[0].shape[1:]
    return pl.pallas_call(
        join_kernel,
        out_shape=jax.ShapeDtypeStruct(shape, BF),
        in_specs=[VMEM] * NY,
        out_specs=VMEM,
        compiler_params=PARAMS,
        name="join",
    )(*levels)


def core_sum_kernel(keep_upper_ref, got_upper_hbm, keep_lower_ref, got_lower_ref, own_ref, *refs):
    send_refs, (got_upper_ref, sem) = refs[: NY - 1], refs[NY - 1 :]
    fetch = pltpu.make_async_copy(got_upper_hbm, got_upper_ref, sem)
    fetch.start()
    for half, (keep_ref, got_ref) in ((1, (keep_lower_ref, got_lower_ref)), (0, (keep_upper_ref, got_upper_ref))):
        if half == 0:
            fetch.wait()
        rows = slice(24 * half, 24 * half + 24)
        for s in range(NY):
            for z in range(NZ):
                total = keep_ref[s, z] + got_ref[s, z].astype(F32)
                if s == 0:
                    own_ref[z, rows] = total
                else:
                    send_refs[s - 1][z, rows] = total.astype(BF)


def y_sum_kernel(own_ref, *refs):
    got_refs, total_ref, send_refs = refs[: NY - 1], refs[NY - 1], refs[NY:]
    for z in range(NZ):
        total = own_ref[z]
        for got_ref in got_refs:
            total = total + got_ref[z].astype(F32)
        if z == 0:
            total_ref[...] = total
        else:
            send_refs[z - 1][...] = total.astype(BF)


def z_sum_kernel(scales, own_ref, *refs):
    got_refs, upper_ref, lower_ref = refs[: NZ - 1], refs[NZ - 1], refs[NZ]
    total = own_ref[...]
    for got_ref in got_refs:
        total = total + got_ref[...].astype(F32)
    lane = lax.broadcasted_iota(jnp.int32, (24, 512), 1)
    for k in range(KWIDTH):
        upper_ref[k] = pltpu.roll(total[0:24], (512 - 96 * k) % 512, 1)[0:22, 0:96] * scales[0]
        lower = pltpu.roll(total[24:48], (512 - 96 * k) % 512, 1)
        packed = lower
        for group in range(1, 4):
            packed = jnp.where(lane >= 22 * group, pltpu.roll(lower, 512 - 2 * group, 1), packed)
        lower_ref[k] = packed[0:20, 0:88] * scales[1]


def small_call(kernel, name, out_shape, *operands):
    return pl.pallas_call(
        kernel,
        out_shape=out_shape,
        in_specs=[VMEM] * len(operands),
        out_specs=tuple(VMEM for _ in out_shape),
        compiler_params=PARAMS,
        name=name,
    )(*operands)


def core_sum(upper, lower):
    level = jax.ShapeDtypeStruct((NZ, 48, 512), BF)
    outs = (jax.ShapeDtypeStruct(level.shape, F32),) + (level,) * (NY - 1)
    got_upper = pltpu.with_memory_space_constraint(upper[1], pltpu.HBM)
    return pl.pallas_call(
        core_sum_kernel,
        out_shape=outs,
        in_specs=[VMEM, HBM, VMEM, VMEM],
        out_specs=tuple(VMEM for _ in outs),
        scratch_shapes=[pltpu.VMEM(got_upper.shape, BF), pltpu.SemaphoreType.DMA(())],
        compiler_params=PARAMS,
        name="core_sum",
    )(upper[0], got_upper, *lower)


def z_sum(own, got, scales, upper_shape, lower_shape):
    block = jax.ShapeDtypeStruct((48, 512), BF)
    own, *sends = small_call(
        y_sum_kernel, "y_sum", (jax.ShapeDtypeStruct(block.shape, F32),) + (block,) * (NZ - 1), own, *got
    )
    got = [shifted(send, "zh", NZ, s + 1) for s, send in enumerate(sends)]
    outs = (jax.ShapeDtypeStruct(upper_shape, F32), jax.ShapeDtypeStruct(lower_shape, F32))
    return small_call(functools.partial(z_sum_kernel, scales), "z_sum", outs, own, *got)


def doubling():
    row = lax.broadcasted_iota(jnp.int32, (128, 256), 0)
    col = lax.broadcasted_iota(jnp.int32, (128, 256), 1)
    return (row == lax.shift_right_logical(col, 1)).astype(F32).astype(BF)


def mm(a, b):
    return jnp.dot(a, b, preferred_element_type=F32)


def one_hot(rows, start, pads):
    row = lax.broadcasted_iota(jnp.int32, (rows, 512), 0)
    col = lax.broadcasted_iota(jnp.int32, (rows, 512), 1)
    place = row + start
    if pads:
        for edge in (22, 44, 66):
            place = place + jnp.where(row >= edge, 2, 0)
    return (place == col).astype(F32).astype(BF)


def pack_kernel(
    tower_hbm, upper_hbm, lower_hbm, pre_upper_hbm, pre_lower_hbm, out_ref, lower_out_ref,
    tower_ref, upper_ref, lower_ref, pre_upper_ref, pre_lower_ref, weight_ref, tower_rows_ref, buf_ref, sem, in_sem,
):
    pieces = [(upper_hbm, upper_ref), (lower_hbm, lower_ref), (tower_hbm, tower_ref)]
    for source, target in ((pre_upper_hbm, pre_upper_ref), (pre_lower_hbm, pre_lower_ref)):
        pieces.append((source.at[:, pl.ds(source.shape[1] - 128, 128)], target.at[0]))
        pieces.append((source.at[:, pl.ds(0, 128)], target.at[1]))
    copies = [pltpu.make_async_copy(source, target, in_sem.at[i]) for i, (source, target) in enumerate(pieces)]
    for copy in copies:
        copy.start()
    for copy in copies:
        copy.wait()
    weight_ref[...] = jnp.zeros((48, 512), F32)
    weight_ref[0:22, :] = sum(mm(upper_ref[k], one_hot(96, 96 * k, False)) for k in range(KWIDTH))
    weight_ref[24:44, :] = sum(mm(lower_ref[k], one_hot(88, 96 * k, True)) for k in range(KWIDTH))
    last, first = (pre_upper_ref[i].astype(F32).T for i in range(2))
    low_last, low_first = (pre_lower_ref[i].astype(F32).T for i in range(2))
    weight_ref[22:24, 0:96] = last[126:128]
    weight_ref[23:24, 128:224] = last[125:126]
    weight_ref[22:24, 256:344] = low_last[126:128]
    tower_rows_ref[...] = jnp.zeros((128, 512), F32)
    for p in range(16):
        tower_rows_ref[8 * p + 6 : 8 * p + 8, 0:96] = first[0:2]
        tower_rows_ref[8 * p + 6 : 8 * p + 7, 128:224] = first[2:3]
        tower_rows_ref[8 * p + 6 : 8 * p + 8, 256:344] = low_first[0:2]
    weight = weight_ref[0:24, :].astype(BF)
    lower_out_ref[...] = weight_ref[24:48, :].astype(BF)
    tower = tower_ref[...].astype(F32)
    for p in range(16):
        at, row = 512 * p, 8 * p
        tower_rows_ref[row : row + 3, :] = tower[:, at : at + 512]
        if p > 0:
            tower_rows_ref[row + 3 : row + 6, 0:128] = tower[:, at - 128 : at]
        tower_rows_ref[row + 3 : row + 6, 128:256] = tower[:, at + 256 : at + 384]
        tower_rows_ref[row + 3 : row + 6, 256:384] = tower[:, at + 128 : at + 256]
        if p < 15:
            tower_rows_ref[row + 3 : row + 6, 384:512] = tower[:, at + 512 : at + 640]
        buf_ref[p, 0:24, :] = weight
        buf_ref[p, 24:32, :] = tower_rows_ref[row : row + 8, :].astype(BF)
        pltpu.make_async_copy(buf_ref.at[p], out_ref.at[p], sem.at[p]).start()
    for p in range(16):
        pltpu.make_async_copy(buf_ref.at[p], out_ref.at[p], sem.at[p]).wait()


def edge_tiles(pos_ref, other_ref, at, deep):
    chip = pos_ref[0] * NY + pos_ref[1]
    before = other_ref[jnp.maximum(chip - 1 + pos_ref[2], 0), 16:24, :].astype(F32)
    after = other_ref[jnp.minimum(chip + pos_ref[2], NZ * NY - 1), 24:32, :].astype(F32)
    row = lax.broadcasted_iota(jnp.int32, (8, 128), 0)
    low = before[:, at : at + 128]
    high = pltpu.roll(after[:, at : at + 128], 2, 0)
    if deep:
        low = jnp.where(row == 5, pltpu.roll(before[:, at + 128 : at + 256], 6, 0), low)
        high = jnp.where(row == 2, pltpu.roll(after[:, at + 128 : at + 256], 4, 0), high)
    rest = jnp.zeros((120, 128), F32)
    return jnp.concatenate([rest, low], axis=0).T, jnp.concatenate([high, rest], axis=0).T


def upper_kernel(
    pos_ref, slope_ref, own_ref, other_ref, mid_ref, taps_out_ref, edge_out_ref,
    main_ref, edge_ref, w_ref, halo_ref, buf_ref, taps_ref, edge_rows_ref, sem,
):
    first = pos_ref[2] == 0
    for p in range(16):
        own, other = own_ref[p, 24:32, :].astype(F32), other_ref[p, 24:32, :].astype(F32)
        for j in range(2):
            rows = jnp.where(first, own, other) if j == 0 else jnp.where(first, other, own)
            rows = jnp.where(first, rows[:, 0:256], rows[:, 256:512])
            at = 3 * (2 * p + j)
            main_ref[at : at + 3, :] = rows[0:3]
            edge_ref[at : at + 3, :] = rows[3:6]
        own, other = own_ref[p, 0:24, :].astype(F32), other_ref[p, 0:24, :].astype(F32)
        both = [jnp.where(first, own, other), jnp.where(first, other, own)]
        w_ref[48 * p : 48 * p + 48, :] = jnp.concatenate(both, axis=0).astype(BF)
    spread = doubling()
    main = main_ref[...].astype(BF)
    edge = edge_ref[...].astype(BF)
    grad = jnp.concatenate(
        [
            mm(edge[:, :128], spread)[:, 128:],
            mm(main[:, :128], spread),
            mm(main[:, 128:], spread),
            mm(edge[:, 128:], spread)[:, :128],
        ],
        axis=1,
    )
    low, high = edge_tiles(pos_ref, other_ref, 0, True)
    slope = jnp.concatenate([half_slope(low[0:96]), slope_ref[...], half_slope(high[0:96])], axis=1)
    grad = grad * slope
    lane = lax.broadcasted_iota(jnp.int32, (96, 128), 1)
    taps_ref[480:512, :] = jnp.zeros((32, 512), BF)
    halo_ref[480:512, :] = jnp.zeros((32, 128), F32)
    for k in range(KWIDTH):
        moved = pltpu.roll(grad, 768 - (130 - k), 1)
        after = pltpu.roll(moved[:, 512:640], 126, 1)
        taps_ref[96 * k : 96 * k + 96, :] = moved[:, 0:512].astype(BF)
        halo_ref[96 * k : 96 * k + 96, :] = jnp.where(lane == 127, moved[:, 640:768], after)
    out_copies = [
        pltpu.make_async_copy(taps_ref, taps_out_ref, sem.at[8]),
        pltpu.make_async_copy(edge_rows_ref, edge_out_ref, sem.at[9]),
    ]
    out_copies[0].start()
    outside = lax.dot_general(
        halo_ref[...].T.astype(BF), w_ref[...], (((1,), (1,)), ((), ())), preferred_element_type=F32
    )[120:128]
    row = lax.broadcasted_iota(jnp.int32, (8, 256), 0)
    for half in range(2):
        lanes = slice(256 * half, 256 * half + 256)
        mid = mm(w_ref[...], taps_ref[:, lanes])
        for d in range(8):
            part = mid[96 * d : 96 * d + 96]
            if half == 0:
                moved = pltpu.roll(outside, (768 - 96 * d) % 768, 1)[:, 0:256]
                part = jnp.concatenate([part[0:16], jnp.where(row >= 6, moved, part[16:24]), part[24:]], axis=0)
            buf_ref[d, :, lanes] = part.astype(BF)
    for d in range(8):
        pltpu.make_async_copy(buf_ref.at[d], mid_ref.at[d], sem.at[d]).start()
    edge_rows_ref[...] = jnp.zeros((96, 256), F32)
    for half, tile in enumerate(edge_tiles(pos_ref, other_ref, 256, False)):
        for group in range(4):
            rows, lanes = slice(24 * group, 24 * group + 22), slice(128 * half, 128 * half + 128)
            edge_rows_ref[rows, lanes] = tile[22 * group : 22 * group + 22]
    out_copies[1].start()
    for d in range(8):
        pltpu.make_async_copy(buf_ref.at[d], mid_ref.at[d], sem.at[d]).wait()
    for copy in out_copies:
        copy.wait()


def lower_weight_kernel(pos_ref, own_ref, other_ref, out_ref, rows_ref):
    first = pos_ref[2] == 0
    for p in range(16):
        slot = lax.rem(pos_ref[1] - p % NY + NY, NY) * NZ + lax.rem(pos_ref[0] - p // NY + NZ, NZ)
        own, other = own_ref[slot].astype(F32), other_ref[slot].astype(F32)
        rows_ref[40 * p : 40 * p + 24, :] = jnp.where(first, own, other)
        rows_ref[40 * p + 20 : 40 * p + 44, :] = jnp.where(first, other, own)
    out_ref[...] = rows_ref[0:640, :].astype(BF)


def lower_taps_kernel(pos_ref, mid_ref, slope_ref, edge_ref, taps_ref):
    place = pos_ref[0] * (NY * NC) + pos_ref[1] * NC + pos_ref[2]
    total = mid_ref[0].astype(F32)
    for d in range(1, 8):
        total = total + mid_ref[d].astype(F32)
    mid = total.astype(BF)
    ends = mid[:, 0:128].astype(F32).T
    left = jnp.broadcast_to(jnp.where(place == 0, 0.0, ends[0:96, 23:24]), (96, 128))
    right = jnp.broadcast_to(jnp.where(place == 31, 0.0, ends[0:96, 22:23]), (96, 128))
    edge = half_slope(edge_ref[...])
    spread = doubling()
    grad = jnp.concatenate([mm(mid[:, 128 * j : 128 * j + 128], spread) for j in range(4)], axis=1)
    grad = jnp.concatenate(
        [left * edge[:, 0:128], grad * slope_ref[...], right * edge[:, 128:256]], axis=1
    )
    taps_ref[480:512, :] = jnp.zeros((32, 1024), BF)
    for k in range(KWIDTH):
        moved = pltpu.roll(grad, 1280 - (130 - k), 1)
        taps_ref[96 * k : 96 * k + 96, :] = moved[:, 0:1024].astype(BF)


def low_kernel(taps_ref, w_ref, low_ref, buf_ref, sem):
    for quarter in range(4):
        lanes = slice(256 * quarter, 256 * quarter + 256)
        low = mm(w_ref[...], taps_ref[:, lanes])
        for d in range(8):
            buf_ref[d, :, lanes] = low[80 * d : 80 * d + 80].astype(BF)
        pltpu.make_async_copy(buf_ref.at[:, :, lanes], low_ref.at[:, :, lanes], sem.at[quarter]).start()
    for quarter in range(4):
        lanes = slice(256 * quarter, 256 * quarter + 256)
        pltpu.make_async_copy(buf_ref.at[:, :, lanes], low_ref.at[:, :, lanes], sem.at[quarter]).wait()


def total_kernel(low_ref, out_ref):
    total = low_ref[0].astype(F32)
    for d in range(1, 8):
        total = total + low_ref[d].astype(F32)
    out_ref[...] = total.astype(BF)


def fetched_weight_grad_kernel(
    pos_ref, act_hbm, taps_hbm, keep_ref, send_ref, rows_ref, block_ref, act_ref, taps_ref, sem
):
    copies = [
        pltpu.make_async_copy(act_hbm, act_ref, sem.at[0]),
        pltpu.make_async_copy(taps_hbm, taps_ref, sem.at[1]),
    ]
    for copy in copies:
        copy.start()
    for copy in copies:
        copy.wait()
    weight_grad_kernel(pos_ref, act_ref, taps_ref, keep_ref, send_ref, rows_ref, block_ref)


def weight_grad_kernel(pos_ref, act_ref, taps_ref, keep_ref, send_ref, rows_ref, block_ref):
    channels, count = act_ref.shape
    width = channels // 32
    rows_ref[channels:, :] = jnp.zeros((8, rows_ref.shape[1]), F32)
    rows_ref[0:channels, :] = lax.dot_general(
        act_ref[...], taps_ref[:, 0:count], (((1,), (1,)), ((), ())), preferred_element_type=F32
    )
    for q in range(32):
        block_ref[q] = rows_ref[width * q : width * q + 24, :]
    for ry in range(NY):
        for rz in range(NZ):
            zh = lax.rem(pos_ref[0] + rz, NZ)
            y = lax.rem(pos_ref[1] + ry, NY)
            base = (zh * NY + y) * NC
            keep_ref[ry, rz] = block_ref[base + pos_ref[2]]
            send_ref[ry, rz] = block_ref[base + 1 - pos_ref[2]].astype(BF)


def weight_grad(pos, act, taps, fetch):
    block = (NY, NZ, 24, taps.shape[0])
    scratch = [pltpu.VMEM((act.shape[0] + 8, taps.shape[0]), F32), pltpu.VMEM((32, 24, taps.shape[0]), F32)]
    if fetch:
        scratch += [pltpu.VMEM(act.shape, BF), pltpu.VMEM(taps.shape, BF), pltpu.SemaphoreType.DMA((2,))]
        act, taps = (pltpu.with_memory_space_constraint(v, pltpu.HBM) for v in (act, taps))
    return pl.pallas_call(
        fetched_weight_grad_kernel if fetch else weight_grad_kernel,
        out_shape=(jax.ShapeDtypeStruct(block, F32), jax.ShapeDtypeStruct(block, BF)),
        in_specs=[SMEM] + [HBM if fetch else VMEM] * 2,
        out_specs=(VMEM, VMEM),
        scratch_shapes=scratch,
        compiler_params=PARAMS,
        name="weight_grad",
    )(pos, act, taps)


def local(tower_grad, act_mid, pre_mid, act_low, pre_low, weight_upper, weight_lower):
    pos = jnp.stack([lax.axis_index("zh"), lax.axis_index("y"), lax.axis_index("c")]).astype(jnp.int32)
    sources = (tower_grad.T, weight_upper, weight_lower, pre_mid.T, pre_low.T)
    packed, lower_block = pl.pallas_call(
        pack_kernel,
        out_shape=(pltpu.HBM((16, 32, 512), BF), jax.ShapeDtypeStruct((24, 512), BF)),
        in_specs=[HBM] * 5,
        out_specs=(HBM, VMEM),
        scratch_shapes=[
            pltpu.VMEM((3, 8192), BF),
            pltpu.VMEM(weight_upper.shape, BF),
            pltpu.VMEM(weight_lower.shape, BF),
            pltpu.VMEM((2, 96, 128), BF),
            pltpu.VMEM((2, 88, 128), BF),
            pltpu.VMEM((48, 512), F32),
            pltpu.VMEM((128, 512), F32),
            pltpu.VMEM((16, 32, 512), BF),
            pltpu.SemaphoreType.DMA((16,)),
            pltpu.SemaphoreType.DMA((7,)),
        ],
        compiler_params=PARAMS,
        name="pack",
    )(*(pltpu.with_memory_space_constraint(v, pltpu.HBM) for v in sources))
    pre_lower = jnp.pad(pre_low.T.reshape(4, 22, 1024), ((0, 0), (0, 2), (0, 0))).reshape(96, 1024)
    slope_upper = half_slope(pre_mid.T)
    slope_lower = half_slope(pre_lower)
    act_low_rows = act_low.T
    lower_blocks = [lower_block] + [shifted(lower_block, "zh", NZ, s) for s in range(1, NZ)]
    own = lax.all_to_all(packed, ("zh", "y"), split_axis=0, concat_axis=0, tiled=True)
    own, slope_upper, slope_lower, act_low_rows, lower_blocks = lax.optimization_barrier(
        (own, slope_upper, slope_lower, act_low_rows, lower_blocks)
    )
    other = shifted(own, "c", NC, 1)

    mid_part, upper_taps, edges = pl.pallas_call(
        upper_kernel,
        out_shape=(pltpu.HBM((8, 96, 512), BF), pltpu.HBM((512, 512), BF), pltpu.HBM((96, 256), F32)),
        in_specs=[SMEM] + [VMEM] * 3,
        out_specs=(HBM, HBM, HBM),
        scratch_shapes=[
            pltpu.VMEM((96, 256), F32),
            pltpu.VMEM((96, 256), F32),
            pltpu.VMEM((768, 512), BF),
            pltpu.VMEM((512, 128), F32),
            pltpu.VMEM((8, 96, 512), BF),
            pltpu.VMEM((512, 512), BF),
            pltpu.VMEM((96, 256), F32),
            pltpu.SemaphoreType.DMA((10,)),
        ],
        compiler_params=PARAMS,
        name="upper",
    )(pos, slope_upper, own, other)
    mid_parts = lax.all_to_all(mid_part, DP, split_axis=0, concat_axis=0, tiled=True)

    lower_blocks, _ = lax.optimization_barrier((lower_blocks, upper_taps))
    lower_level = jnp.stack(lower_blocks)
    lower_levels = [lower_level] + [shifted(lower_level, "y", NY, s) for s in range(1, NY)]
    upper_keep, upper_send = weight_grad(pos, act_mid.T, upper_taps, True)
    lower_levels, upper_send = lax.optimization_barrier((lower_levels, upper_send))
    lower_own = join(lower_levels)
    lower_own, upper_send = lax.optimization_barrier((lower_own, upper_send))
    upper_got = shifted(upper_send, "c", NC, 1)
    lower_other = shifted(lower_own, "c", NC, 1)
    lower_full = pl.pallas_call(
        lower_weight_kernel,
        out_shape=jax.ShapeDtypeStruct((640, 512), BF),
        in_specs=[SMEM] + [VMEM] * 2,
        out_specs=VMEM,
        scratch_shapes=[pltpu.VMEM((648, 512), F32)],
        compiler_params=PARAMS,
        name="lower_weight",
    )(pos, lower_own, lower_other)

    mid_parts, upper_got = lax.optimization_barrier((mid_parts, upper_got))
    lower_taps = pl.pallas_call(
        lower_taps_kernel,
        out_shape=jax.ShapeDtypeStruct((512, 1024), BF),
        in_specs=[SMEM] + [VMEM] * 3,
        out_specs=VMEM,
        compiler_params=PARAMS,
        name="lower_taps",
    )(pos, mid_parts, slope_lower, edges)
    lower_keep, lower_send = weight_grad(pos, act_low_rows, lower_taps, False)
    lower_got = shifted(lower_send, "c", NC, 1)
    own_sum, *sends = core_sum((upper_keep, upper_got), (lower_keep, lower_got))
    lower_taps, _ = lax.optimization_barrier((lower_taps, lower_keep))
    low_part = pl.pallas_call(
        low_kernel,
        out_shape=pltpu.HBM((8, 80, 1024), BF),
        in_specs=[VMEM] * 2,
        out_specs=HBM,
        scratch_shapes=[pltpu.VMEM((8, 80, 1024), BF), pltpu.SemaphoreType.DMA((4,))],
        compiler_params=PARAMS,
        name="low",
    )(lower_taps, lower_full)
    low_part, _ = lax.optimization_barrier((low_part, lower_got))
    low_parts = lax.all_to_all(low_part, DP, split_axis=0, concat_axis=0, tiled=True)
    got = [shifted(send, "y", NY, s + 1) for s, send in enumerate(sends)]
    scales = tuple(1.0 / math.sqrt(act.shape[0] * NZ * NY * NC) for act in (act_mid, act_low))
    grad_upper, grad_lower = z_sum(own_sum, got, scales, weight_upper.shape, weight_lower.shape)

    low_grad = pl.pallas_call(
        total_kernel,
        out_shape=jax.ShapeDtypeStruct((80, 1024), BF),
        in_specs=[VMEM],
        out_specs=VMEM,
        compiler_params=PARAMS,
        name="low_total",
    )(low_parts).T
    return low_grad, grad_upper, grad_lower


def solution(mesh):
    fine = Mesh(mesh.devices.reshape(4, 2, NZ, NY, NC), DP + SEQ)
    in_specs = (
        P(None, DP + SEQ),
        P(SEQ, None),
        P(SEQ, DP),
        P(SEQ, None),
        P(SEQ, DP),
        P(None, SEQ, DP),
        P(None, SEQ, DP),
    )
    out_specs = (P(SEQ, DP), P(None, SEQ, DP), P(None, SEQ, DP))
    return jax.shard_map(local, mesh=fine, in_specs=in_specs, out_specs=out_specs, check_vma=False)
```

```python
import functools
import math

import jax
import jax.numpy as jnp
from jax import lax
from jax.experimental import pallas as pl
from jax.experimental.pallas import tpu as pltpu
from jax.sharding import Mesh, PartitionSpec as P

KWIDTH = 5
HALF = 2
DP = ("x", "zl")
SEQ = ("zh", "y", "c")
NZ, NY, NC = 4, 4, 2
BF = jnp.bfloat16
F32 = jnp.float32
PARAMS = pltpu.CompilerParams(vmem_limit_bytes=16 * 1024 * 1024)
VMEM = pl.BlockSpec(memory_space=pltpu.VMEM)
SMEM = pl.BlockSpec(memory_space=pltpu.SMEM)
HBM = pl.BlockSpec(memory_space=pltpu.HBM)


def half_slope(pre_act):
    values = pre_act.astype(F32)
    cumulative = 0.5 * (1.0 + lax.erf(values * (1.0 / math.sqrt(2.0))))
    density = jnp.exp(-0.5 * values * values) * (1.0 / math.sqrt(2.0 * math.pi))
    return 0.5 * (cumulative + values * density)


def shifted(block, axis, count, step):
    return lax.ppermute(block, axis, [(i, (i + step) % count) for i in range(count)])


def join_kernel(*refs):
    out_ref = refs[-1]
    for s in range(NY):
        out_ref[NZ * s : NZ * s + NZ] = refs[s][...]


def join(levels):
    shape = (NY * NZ,) + levels[0].shape[1:]
    return pl.pallas_call(
        join_kernel,
        out_shape=jax.ShapeDtypeStruct(shape, BF),
        in_specs=[VMEM] * NY,
        out_specs=VMEM,
        compiler_params=PARAMS,
        name="join",
    )(*levels)


def core_sum_kernel(keep_upper_ref, got_upper_hbm, keep_lower_ref, got_lower_ref, own_ref, *refs):
    send_refs, (got_upper_ref, sem) = refs[: NY - 1], refs[NY - 1 :]
    fetch = pltpu.make_async_copy(got_upper_hbm, got_upper_ref, sem)
    fetch.start()
    for half, (keep_ref, got_ref) in ((1, (keep_lower_ref, got_lower_ref)), (0, (keep_upper_ref, got_upper_ref))):
        if half == 0:
            fetch.wait()
        rows = slice(24 * half, 24 * half + 24)
        for s in range(NY):
            for z in range(NZ):
                total = keep_ref[s, z] + got_ref[s, z].astype(F32)
                if s == 0:
                    own_ref[z, rows] = total
                else:
                    send_refs[s - 1][z, rows] = total.astype(BF)


def y_sum_kernel(own_ref, *refs):
    got_refs, total_ref, send_refs = refs[: NY - 1], refs[NY - 1], refs[NY:]
    for z in range(NZ):
        total = own_ref[z]
        for got_ref in got_refs:
            total = total + got_ref[z].astype(F32)
        if z == 0:
            total_ref[...] = total
        else:
            send_refs[z - 1][...] = total.astype(BF)


def z_sum_kernel(scales, own_ref, *refs):
    got_refs, upper_ref, lower_ref = refs[: NZ - 1], refs[NZ - 1], refs[NZ]
    total = own_ref[...]
    for got_ref in got_refs:
        total = total + got_ref[...].astype(F32)
    lane = lax.broadcasted_iota(jnp.int32, (24, 512), 1)
    for k in range(KWIDTH):
        upper_ref[k] = pltpu.roll(total[0:24], (512 - 96 * k) % 512, 1)[0:22, 0:96] * scales[0]
        lower = pltpu.roll(total[24:48], (512 - 96 * k) % 512, 1)
        packed = lower
        for group in range(1, 4):
            packed = jnp.where(lane >= 22 * group, pltpu.roll(lower, 512 - 2 * group, 1), packed)
        lower_ref[k] = packed[0:20, 0:88] * scales[1]


def small_call(kernel, name, out_shape, *operands):
    return pl.pallas_call(
        kernel,
        out_shape=out_shape,
        in_specs=[VMEM] * len(operands),
        out_specs=tuple(VMEM for _ in out_shape),
        compiler_params=PARAMS,
        name=name,
    )(*operands)


def core_sum(upper, lower):
    level = jax.ShapeDtypeStruct((NZ, 48, 512), BF)
    outs = (jax.ShapeDtypeStruct(level.shape, F32),) + (level,) * (NY - 1)
    got_upper = pltpu.with_memory_space_constraint(upper[1], pltpu.HBM)
    return pl.pallas_call(
        core_sum_kernel,
        out_shape=outs,
        in_specs=[VMEM, HBM, VMEM, VMEM],
        out_specs=tuple(VMEM for _ in outs),
        scratch_shapes=[pltpu.VMEM(got_upper.shape, BF), pltpu.SemaphoreType.DMA(())],
        compiler_params=PARAMS,
        name="core_sum",
    )(upper[0], got_upper, *lower)


def z_sum(own, got, low_grad, scales, upper_shape, lower_shape):
    block = jax.ShapeDtypeStruct((48, 512), BF)
    own, *sends = small_call(
        y_sum_kernel, "y_sum", (jax.ShapeDtypeStruct(block.shape, F32),) + (block,) * (NZ - 1), own, *got
    )
    got = [shifted(send, "zh", NZ, s + 1) for s, send in enumerate(sends)]
    got, low_grad = lax.optimization_barrier((got, low_grad))
    outs = (jax.ShapeDtypeStruct(upper_shape, F32), jax.ShapeDtypeStruct(lower_shape, F32))
    return low_grad, *small_call(functools.partial(z_sum_kernel, scales), "z_sum", outs, own, *got)


def doubling():
    row = lax.broadcasted_iota(jnp.int32, (128, 256), 0)
    col = lax.broadcasted_iota(jnp.int32, (128, 256), 1)
    return (row == lax.shift_right_logical(col, 1)).astype(F32).astype(BF)


def mm(a, b):
    return jnp.dot(a, b, preferred_element_type=F32)


def one_hot(rows, start, pads):
    row = lax.broadcasted_iota(jnp.int32, (rows, 512), 0)
    col = lax.broadcasted_iota(jnp.int32, (rows, 512), 1)
    place = row + start
    if pads:
        for edge in (22, 44, 66):
            place = place + jnp.where(row >= edge, 2, 0)
    return (place == col).astype(F32).astype(BF)


def pack_kernel(
    tower_hbm, upper_hbm, lower_hbm, pre_upper_hbm, pre_lower_hbm, out_ref, lower_out_ref,
    tower_ref, upper_ref, lower_ref, pre_upper_ref, pre_lower_ref, weight_ref, tower_rows_ref, buf_ref, sem, in_sem,
):
    pieces = [(upper_hbm, upper_ref), (lower_hbm, lower_ref), (tower_hbm, tower_ref)]
    for source, target in ((pre_upper_hbm, pre_upper_ref), (pre_lower_hbm, pre_lower_ref)):
        pieces.append((source.at[:, pl.ds(source.shape[1] - 128, 128)], target.at[0]))
        pieces.append((source.at[:, pl.ds(0, 128)], target.at[1]))
    copies = [pltpu.make_async_copy(source, target, in_sem.at[i]) for i, (source, target) in enumerate(pieces)]
    for copy in copies:
        copy.start()
    for copy in copies[:1] + copies[2:]:
        copy.wait()
    weight_ref[...] = jnp.zeros((48, 512), F32)
    weight_ref[0:22, :] = sum(mm(upper_ref[k], one_hot(96, 96 * k, False)) for k in range(KWIDTH))
    last, first = (pre_upper_ref[i].astype(F32).T for i in range(2))
    low_last, low_first = (pre_lower_ref[i].astype(F32).T for i in range(2))
    weight_ref[22:24, 0:96] = last[126:128]
    weight_ref[23:24, 128:224] = last[125:126]
    weight_ref[22:24, 256:344] = low_last[126:128]
    tower_rows_ref[...] = jnp.zeros((128, 512), F32)
    for p in range(16):
        tower_rows_ref[8 * p + 6 : 8 * p + 8, 0:96] = first[0:2]
        tower_rows_ref[8 * p + 6 : 8 * p + 7, 128:224] = first[2:3]
        tower_rows_ref[8 * p + 6 : 8 * p + 8, 256:344] = low_first[0:2]
    weight = weight_ref[0:24, :].astype(BF)
    tower = tower_ref[...].astype(F32)
    for p in range(16):
        at, row = 512 * p, 8 * p
        tower_rows_ref[row : row + 3, :] = tower[:, at : at + 512]
        if p > 0:
            tower_rows_ref[row + 3 : row + 6, 0:128] = tower[:, at - 128 : at]
        tower_rows_ref[row + 3 : row + 6, 128:256] = tower[:, at + 256 : at + 384]
        tower_rows_ref[row + 3 : row + 6, 256:384] = tower[:, at + 128 : at + 256]
        if p < 15:
            tower_rows_ref[row + 3 : row + 6, 384:512] = tower[:, at + 512 : at + 640]
        buf_ref[p, 0:24, :] = weight
        buf_ref[p, 24:32, :] = tower_rows_ref[row : row + 8, :].astype(BF)
        pltpu.make_async_copy(buf_ref.at[p], out_ref.at[p], sem.at[p]).start()
    copies[1].wait()
    weight_ref[24:44, :] = sum(mm(lower_ref[k], one_hot(88, 96 * k, True)) for k in range(KWIDTH))
    lower_out_ref[...] = weight_ref[24:48, :].astype(BF)
    for p in range(16):
        pltpu.make_async_copy(buf_ref.at[p], out_ref.at[p], sem.at[p]).wait()


def edge_tiles(pos_ref, other_ref, at, deep):
    chip = pos_ref[0] * NY + pos_ref[1]
    before = other_ref[jnp.maximum(chip - 1 + pos_ref[2], 0), 16:24, :].astype(F32)
    after = other_ref[jnp.minimum(chip + pos_ref[2], NZ * NY - 1), 24:32, :].astype(F32)
    row = lax.broadcasted_iota(jnp.int32, (8, 128), 0)
    low = before[:, at : at + 128]
    high = pltpu.roll(after[:, at : at + 128], 2, 0)
    if deep:
        low = jnp.where(row == 5, pltpu.roll(before[:, at + 128 : at + 256], 6, 0), low)
        high = jnp.where(row == 2, pltpu.roll(after[:, at + 128 : at + 256], 4, 0), high)
    rest = jnp.zeros((120, 128), F32)
    return jnp.concatenate([rest, low], axis=0).T, jnp.concatenate([high, rest], axis=0).T


def upper_kernel(
    pos_ref, slope_ref, own_ref, other_ref, mid_ref, taps_out_ref, edge_out_ref,
    main_ref, edge_ref, w_ref, halo_ref, buf_ref, taps_ref, edge_rows_ref, sem,
):
    first = pos_ref[2] == 0
    for p in range(16):
        own, other = own_ref[p, 24:32, :].astype(F32), other_ref[p, 24:32, :].astype(F32)
        for j in range(2):
            rows = jnp.where(first, own, other) if j == 0 else jnp.where(first, other, own)
            rows = jnp.where(first, rows[:, 0:256], rows[:, 256:512])
            at = 3 * (2 * p + j)
            main_ref[at : at + 3, :] = rows[0:3]
            edge_ref[at : at + 3, :] = rows[3:6]
        own, other = own_ref[p, 0:24, :].astype(F32), other_ref[p, 0:24, :].astype(F32)
        both = [jnp.where(first, own, other), jnp.where(first, other, own)]
        w_ref[48 * p : 48 * p + 48, :] = jnp.concatenate(both, axis=0).astype(BF)
    spread = doubling()
    main = main_ref[...].astype(BF)
    edge = edge_ref[...].astype(BF)
    grad = jnp.concatenate(
        [
            mm(edge[:, :128], spread)[:, 128:],
            mm(main[:, :128], spread),
            mm(main[:, 128:], spread),
            mm(edge[:, 128:], spread)[:, :128],
        ],
        axis=1,
    )
    low, high = edge_tiles(pos_ref, other_ref, 0, True)
    slope = jnp.concatenate([half_slope(low[0:96]), slope_ref[...], half_slope(high[0:96])], axis=1)
    grad = grad * slope
    lane = lax.broadcasted_iota(jnp.int32, (96, 128), 1)
    taps_ref[480:512, :] = jnp.zeros((32, 512), BF)
    halo_ref[480:512, :] = jnp.zeros((32, 128), F32)
    for k in range(KWIDTH):
        moved = pltpu.roll(grad, 768 - (130 - k), 1)
        after = pltpu.roll(moved[:, 512:640], 126, 1)
        taps_ref[96 * k : 96 * k + 96, :] = moved[:, 0:512].astype(BF)
        halo_ref[96 * k : 96 * k + 96, :] = jnp.where(lane == 127, moved[:, 640:768], after)
    out_copies = [
        pltpu.make_async_copy(taps_ref, taps_out_ref, sem.at[2]),
        pltpu.make_async_copy(edge_rows_ref, edge_out_ref, sem.at[3]),
    ]
    out_copies[0].start()
    outside = lax.dot_general(
        halo_ref[...].T.astype(BF), w_ref[...], (((1,), (1,)), ((), ())), preferred_element_type=F32
    )[120:128]
    row = lax.broadcasted_iota(jnp.int32, (8, 256), 0)
    for half in range(2):
        lanes = slice(256 * half, 256 * half + 256)
        mid = mm(w_ref[...], taps_ref[:, lanes])
        for d in range(8):
            part = mid[96 * d : 96 * d + 96]
            if half == 0:
                moved = pltpu.roll(outside, (768 - 96 * d) % 768, 1)[:, 0:256]
                part = jnp.concatenate([part[0:16], jnp.where(row >= 6, moved, part[16:24]), part[24:]], axis=0)
            buf_ref[d, :, lanes] = part.astype(BF)
        out_copies.append(pltpu.make_async_copy(buf_ref.at[:, :, lanes], mid_ref.at[:, :, lanes], sem.at[half]))
        out_copies[-1].start()
    edge_rows_ref[...] = jnp.zeros((96, 256), F32)
    for half, tile in enumerate(edge_tiles(pos_ref, other_ref, 256, False)):
        for group in range(4):
            rows, lanes = slice(24 * group, 24 * group + 22), slice(128 * half, 128 * half + 128)
            edge_rows_ref[rows, lanes] = tile[22 * group : 22 * group + 22]
    out_copies[1].start()
    for copy in out_copies:
        copy.wait()


def lower_weight_kernel(pos_ref, own_ref, other_ref, out_ref, rows_ref):
    first = pos_ref[2] == 0
    for p in range(16):
        slot = lax.rem(pos_ref[1] - p % NY + NY, NY) * NZ + lax.rem(pos_ref[0] - p // NY + NZ, NZ)
        own, other = own_ref[slot].astype(F32), other_ref[slot].astype(F32)
        rows_ref[40 * p : 40 * p + 24, :] = jnp.where(first, own, other)
        rows_ref[40 * p + 20 : 40 * p + 44, :] = jnp.where(first, other, own)
    out_ref[...] = rows_ref[0:640, :].astype(BF)


def lower_taps_kernel(pos_ref, mid_ref, slope_ref, edge_ref, taps_ref):
    place = pos_ref[0] * (NY * NC) + pos_ref[1] * NC + pos_ref[2]
    total = mid_ref[0].astype(F32)
    for d in range(1, 8):
        total = total + mid_ref[d].astype(F32)
    mid = total.astype(BF)
    ends = mid[:, 0:128].astype(F32).T
    left = jnp.broadcast_to(jnp.where(place == 0, 0.0, ends[0:96, 23:24]), (96, 128))
    right = jnp.broadcast_to(jnp.where(place == 31, 0.0, ends[0:96, 22:23]), (96, 128))
    edge = half_slope(edge_ref[...])
    spread = doubling()
    grad = jnp.concatenate([mm(mid[:, 128 * j : 128 * j + 128], spread) for j in range(4)], axis=1)
    grad = jnp.concatenate(
        [left * edge[:, 0:128], grad * slope_ref[...], right * edge[:, 128:256]], axis=1
    )
    taps_ref[480:512, :] = jnp.zeros((32, 1024), BF)
    for k in range(KWIDTH):
        moved = pltpu.roll(grad, 1280 - (130 - k), 1)
        taps_ref[96 * k : 96 * k + 96, :] = moved[:, 0:1024].astype(BF)


def low_kernel(taps_ref, w_ref, low_ref, buf_ref, sem):
    for quarter in range(4):
        lanes = slice(256 * quarter, 256 * quarter + 256)
        low = mm(w_ref[...], taps_ref[:, lanes])
        for d in range(8):
            buf_ref[d, :, lanes] = low[80 * d : 80 * d + 80].astype(BF)
        pltpu.make_async_copy(buf_ref.at[:, :, lanes], low_ref.at[:, :, lanes], sem.at[quarter]).start()
    for quarter in range(4):
        lanes = slice(256 * quarter, 256 * quarter + 256)
        pltpu.make_async_copy(buf_ref.at[:, :, lanes], low_ref.at[:, :, lanes], sem.at[quarter]).wait()


def total_kernel(low_ref, out_ref):
    total = low_ref[0].astype(F32)
    for d in range(1, 8):
        total = total + low_ref[d].astype(F32)
    out_ref[...] = total.astype(BF)


def fetched_weight_grad_kernel(
    pos_ref, act_hbm, taps_hbm, keep_ref, send_ref, rows_ref, block_ref, act_ref, taps_ref, sem
):
    copies = [
        pltpu.make_async_copy(act_hbm, act_ref, sem.at[0]),
        pltpu.make_async_copy(taps_hbm, taps_ref, sem.at[1]),
    ]
    for copy in copies:
        copy.start()
    for copy in copies:
        copy.wait()
    weight_grad_kernel(pos_ref, act_ref, taps_ref, keep_ref, send_ref, rows_ref, block_ref)


def weight_grad_kernel(pos_ref, act_ref, taps_ref, keep_ref, send_ref, rows_ref, block_ref):
    channels, count = act_ref.shape
    width = channels // 32
    rows_ref[channels:, :] = jnp.zeros((8, rows_ref.shape[1]), F32)
    rows_ref[0:channels, :] = lax.dot_general(
        act_ref[...], taps_ref[:, 0:count], (((1,), (1,)), ((), ())), preferred_element_type=F32
    )
    for q in range(32):
        block_ref[q] = rows_ref[width * q : width * q + 24, :]
    for ry in range(NY):
        for rz in range(NZ):
            zh = lax.rem(pos_ref[0] + rz, NZ)
            y = lax.rem(pos_ref[1] + ry, NY)
            base = (zh * NY + y) * NC
            keep_ref[ry, rz] = block_ref[base + pos_ref[2]]
            send_ref[ry, rz] = block_ref[base + 1 - pos_ref[2]].astype(BF)


def weight_grad(pos, act, taps, fetch):
    block = (NY, NZ, 24, taps.shape[0])
    scratch = [pltpu.VMEM((act.shape[0] + 8, taps.shape[0]), F32), pltpu.VMEM((32, 24, taps.shape[0]), F32)]
    if fetch:
        scratch += [pltpu.VMEM(act.shape, BF), pltpu.VMEM(taps.shape, BF), pltpu.SemaphoreType.DMA((2,))]
        act, taps = (pltpu.with_memory_space_constraint(v, pltpu.HBM) for v in (act, taps))
    return pl.pallas_call(
        fetched_weight_grad_kernel if fetch else weight_grad_kernel,
        out_shape=(jax.ShapeDtypeStruct(block, F32), jax.ShapeDtypeStruct(block, BF)),
        in_specs=[SMEM] + [HBM if fetch else VMEM] * 2,
        out_specs=(VMEM, VMEM),
        scratch_shapes=scratch,
        compiler_params=PARAMS,
        name="weight_grad",
    )(pos, act, taps)


def local(tower_grad, act_mid, pre_mid, act_low, pre_low, weight_upper, weight_lower):
    pos = jnp.stack([lax.axis_index("zh"), lax.axis_index("y"), lax.axis_index("c")]).astype(jnp.int32)
    sources = (tower_grad.T, weight_upper, weight_lower, pre_mid.T, pre_low.T)
    packed, lower_block = pl.pallas_call(
        pack_kernel,
        out_shape=(pltpu.HBM((16, 32, 512), BF), jax.ShapeDtypeStruct((24, 512), BF)),
        in_specs=[HBM] * 5,
        out_specs=(HBM, VMEM),
        scratch_shapes=[
            pltpu.VMEM((3, 8192), BF),
            pltpu.VMEM(weight_upper.shape, BF),
            pltpu.VMEM(weight_lower.shape, BF),
            pltpu.VMEM((2, 96, 128), BF),
            pltpu.VMEM((2, 88, 128), BF),
            pltpu.VMEM((48, 512), F32),
            pltpu.VMEM((128, 512), F32),
            pltpu.VMEM((16, 32, 512), BF),
            pltpu.SemaphoreType.DMA((16,)),
            pltpu.SemaphoreType.DMA((7,)),
        ],
        compiler_params=PARAMS,
        name="pack",
    )(*(pltpu.with_memory_space_constraint(v, pltpu.HBM) for v in sources))
    pre_lower = jnp.pad(pre_low.T.reshape(4, 22, 1024), ((0, 0), (0, 2), (0, 0))).reshape(96, 1024)
    slope_upper = half_slope(pre_mid.T)
    slope_lower = half_slope(pre_lower)
    act_low_rows = act_low.T
    lower_blocks = [lower_block] + [shifted(lower_block, "zh", NZ, s) for s in range(1, NZ)]
    own = lax.all_to_all(packed, ("zh", "y"), split_axis=0, concat_axis=0, tiled=True)
    own, slope_upper, slope_lower, act_low_rows, lower_blocks = lax.optimization_barrier(
        (own, slope_upper, slope_lower, act_low_rows, lower_blocks)
    )
    other = shifted(own, "c", NC, 1)

    mid_part, upper_taps, edges = pl.pallas_call(
        upper_kernel,
        out_shape=(pltpu.HBM((8, 96, 512), BF), pltpu.HBM((512, 512), BF), pltpu.HBM((96, 256), F32)),
        in_specs=[SMEM] + [VMEM] * 3,
        out_specs=(HBM, HBM, HBM),
        scratch_shapes=[
            pltpu.VMEM((96, 256), F32),
            pltpu.VMEM((96, 256), F32),
            pltpu.VMEM((768, 512), BF),
            pltpu.VMEM((512, 128), F32),
            pltpu.VMEM((8, 96, 512), BF),
            pltpu.VMEM((512, 512), BF),
            pltpu.VMEM((96, 256), F32),
            pltpu.SemaphoreType.DMA((4,)),
        ],
        compiler_params=PARAMS,
        name="upper",
    )(pos, slope_upper, own, other)
    mid_parts = lax.all_to_all(mid_part, DP, split_axis=0, concat_axis=0, tiled=True)

    lower_blocks, _ = lax.optimization_barrier((lower_blocks, upper_taps))
    lower_level = jnp.stack(lower_blocks)
    lower_levels = [lower_level] + [shifted(lower_level, "y", NY, s) for s in range(1, NY)]
    upper_keep, upper_send = weight_grad(pos, act_mid.T, upper_taps, True)
    lower_levels, upper_send = lax.optimization_barrier((lower_levels, upper_send))
    lower_own = join(lower_levels)
    lower_own, upper_send = lax.optimization_barrier((lower_own, upper_send))
    upper_got = shifted(upper_send, "c", NC, 1)
    lower_other = shifted(lower_own, "c", NC, 1)
    lower_full = pl.pallas_call(
        lower_weight_kernel,
        out_shape=jax.ShapeDtypeStruct((640, 512), BF),
        in_specs=[SMEM] + [VMEM] * 2,
        out_specs=VMEM,
        scratch_shapes=[pltpu.VMEM((648, 512), F32)],
        compiler_params=PARAMS,
        name="lower_weight",
    )(pos, lower_own, lower_other)

    mid_parts, upper_got = lax.optimization_barrier((mid_parts, upper_got))
    lower_taps = pl.pallas_call(
        lower_taps_kernel,
        out_shape=jax.ShapeDtypeStruct((512, 1024), BF),
        in_specs=[SMEM] + [VMEM] * 3,
        out_specs=VMEM,
        compiler_params=PARAMS,
        name="lower_taps",
    )(pos, mid_parts, slope_lower, edges)
    lower_keep, lower_send = weight_grad(pos, act_low_rows, lower_taps, False)
    lower_got = shifted(lower_send, "c", NC, 1)
    own_sum, *sends = core_sum((upper_keep, upper_got), (lower_keep, lower_got))
    lower_taps, _ = lax.optimization_barrier((lower_taps, lower_keep))
    low_part = pl.pallas_call(
        low_kernel,
        out_shape=pltpu.HBM((8, 80, 1024), BF),
        in_specs=[VMEM] * 2,
        out_specs=HBM,
        scratch_shapes=[pltpu.VMEM((8, 80, 1024), BF), pltpu.SemaphoreType.DMA((4,))],
        compiler_params=PARAMS,
        name="low",
    )(lower_taps, lower_full)
    low_part, _ = lax.optimization_barrier((low_part, lower_got))
    low_parts = lax.all_to_all(low_part, DP, split_axis=0, concat_axis=0, tiled=True)
    got = [shifted(send, "y", NY, s + 1) for s, send in enumerate(sends)]
    low_grad = pl.pallas_call(
        total_kernel,
        out_shape=jax.ShapeDtypeStruct((80, 1024), BF),
        in_specs=[VMEM],
        out_specs=VMEM,
        compiler_params=PARAMS,
        name="low_total",
    )(low_parts)
    scales = tuple(1.0 / math.sqrt(act.shape[0] * NZ * NY * NC) for act in (act_mid, act_low))
    low_grad, grad_upper, grad_lower = z_sum(own_sum, got, low_grad, scales, weight_upper.shape, weight_lower.shape)
    return low_grad.T, grad_upper, grad_lower


def solution(mesh):
    fine = Mesh(mesh.devices.reshape(4, 2, NZ, NY, NC), DP + SEQ)
    in_specs = (
        P(None, DP + SEQ),
        P(SEQ, None),
        P(SEQ, DP),
        P(SEQ, None),
        P(SEQ, DP),
        P(None, SEQ, DP),
        P(None, SEQ, DP),
    )
    out_specs = (P(SEQ, DP), P(None, SEQ, DP), P(None, SEQ, DP))
    return jax.shard_map(local, mesh=fine, in_specs=in_specs, out_specs=out_specs, check_vma=False)
```

```python
import functools
import math

import jax
import jax.numpy as jnp
from jax import lax
from jax.experimental import pallas as pl
from jax.experimental.pallas import tpu as pltpu
from jax.sharding import Mesh, PartitionSpec as P

KWIDTH = 5
HALF = 2
DP = ("x", "zl")
SEQ = ("zh", "y", "c")
NZ, NY, NC = 4, 4, 2
BF = jnp.bfloat16
F32 = jnp.float32
PARAMS = pltpu.CompilerParams(vmem_limit_bytes=16 * 1024 * 1024)
VMEM = pl.BlockSpec(memory_space=pltpu.VMEM)
SMEM = pl.BlockSpec(memory_space=pltpu.SMEM)
HBM = pl.BlockSpec(memory_space=pltpu.HBM)


def half_slope(pre_act):
    values = pre_act.astype(F32)
    cumulative = 0.5 * (1.0 + lax.erf(values * (1.0 / math.sqrt(2.0))))
    density = jnp.exp(-0.5 * values * values) * (1.0 / math.sqrt(2.0 * math.pi))
    return 0.5 * (cumulative + values * density)


def shifted(block, axis, count, step):
    return lax.ppermute(block, axis, [(i, (i + step) % count) for i in range(count)])


def join_kernel(*refs):
    out_ref = refs[-1]
    for s in range(NY):
        out_ref[NZ * s : NZ * s + NZ] = refs[s][...]


def join(levels):
    shape = (NY * NZ,) + levels[0].shape[1:]
    return pl.pallas_call(
        join_kernel,
        out_shape=jax.ShapeDtypeStruct(shape, BF),
        in_specs=[VMEM] * NY,
        out_specs=VMEM,
        compiler_params=PARAMS,
        name="join",
    )(*levels)


def core_sum_kernel(keep_upper_ref, got_upper_hbm, keep_lower_ref, got_lower_ref, own_ref, *refs):
    send_refs, (got_upper_ref, sem) = refs[: NY - 1], refs[NY - 1 :]
    fetch = pltpu.make_async_copy(got_upper_hbm, got_upper_ref, sem)
    fetch.start()
    for half, (keep_ref, got_ref) in ((1, (keep_lower_ref, got_lower_ref)), (0, (keep_upper_ref, got_upper_ref))):
        if half == 0:
            fetch.wait()
        rows = slice(24 * half, 24 * half + 24)
        for s in range(NY):
            for z in range(NZ):
                total = keep_ref[s, z] + got_ref[s, z].astype(F32)
                if s == 0:
                    own_ref[z, rows] = total
                else:
                    send_refs[s - 1][z, rows] = total.astype(BF)


def y_sum_kernel(own_ref, *refs):
    got_refs, total_ref, send_refs = refs[: NY - 1], refs[NY - 1], refs[NY:]
    for z in range(NZ):
        total = own_ref[z]
        for got_ref in got_refs:
            total = total + got_ref[z].astype(F32)
        if z == 0:
            total_ref[...] = total
        else:
            send_refs[z - 1][...] = total.astype(BF)


def z_sum_kernel(scales, own_ref, *refs):
    got_refs, upper_ref, lower_ref = refs[: NZ - 1], refs[NZ - 1], refs[NZ]
    total = own_ref[...]
    for got_ref in got_refs:
        total = total + got_ref[...].astype(F32)
    lane = lax.broadcasted_iota(jnp.int32, (24, 512), 1)
    for k in range(KWIDTH):
        upper_ref[k] = pltpu.roll(total[0:24], (512 - 96 * k) % 512, 1)[0:22, 0:96] * scales[0]
        lower = pltpu.roll(total[24:48], (512 - 96 * k) % 512, 1)
        packed = lower
        for group in range(1, 4):
            packed = jnp.where(lane >= 22 * group, pltpu.roll(lower, 512 - 2 * group, 1), packed)
        lower_ref[k] = packed[0:20, 0:88] * scales[1]


def small_call(kernel, name, out_shape, *operands):
    return pl.pallas_call(
        kernel,
        out_shape=out_shape,
        in_specs=[VMEM] * len(operands),
        out_specs=tuple(VMEM for _ in out_shape),
        compiler_params=PARAMS,
        name=name,
    )(*operands)


def core_sum(upper, lower):
    level = jax.ShapeDtypeStruct((NZ, 48, 512), BF)
    outs = (jax.ShapeDtypeStruct(level.shape, F32),) + (level,) * (NY - 1)
    got_upper = pltpu.with_memory_space_constraint(upper[1], pltpu.HBM)
    return pl.pallas_call(
        core_sum_kernel,
        out_shape=outs,
        in_specs=[VMEM, HBM, VMEM, VMEM],
        out_specs=tuple(VMEM for _ in outs),
        scratch_shapes=[pltpu.VMEM(got_upper.shape, BF), pltpu.SemaphoreType.DMA(())],
        compiler_params=PARAMS,
        name="core_sum",
    )(upper[0], got_upper, *lower)


def z_sum(own, got, low_grad, scales, upper_shape, lower_shape):
    block = jax.ShapeDtypeStruct((48, 512), BF)
    own, *sends = small_call(
        y_sum_kernel, "y_sum", (jax.ShapeDtypeStruct(block.shape, F32),) + (block,) * (NZ - 1), own, *got
    )
    got = [shifted(send, "zh", NZ, s + 1) for s, send in enumerate(sends)]
    got, low_grad = lax.optimization_barrier((got, low_grad))
    outs = (jax.ShapeDtypeStruct(upper_shape, F32), jax.ShapeDtypeStruct(lower_shape, F32))
    return low_grad, *small_call(functools.partial(z_sum_kernel, scales), "z_sum", outs, own, *got)


def doubling():
    row = lax.broadcasted_iota(jnp.int32, (128, 256), 0)
    col = lax.broadcasted_iota(jnp.int32, (128, 256), 1)
    return (row == lax.shift_right_logical(col, 1)).astype(F32).astype(BF)


def mm(a, b):
    return jnp.dot(a, b, preferred_element_type=F32)


def one_hot(rows, start, pads):
    row = lax.broadcasted_iota(jnp.int32, (rows, 512), 0)
    col = lax.broadcasted_iota(jnp.int32, (rows, 512), 1)
    place = row + start
    if pads:
        for edge in (22, 44, 66):
            place = place + jnp.where(row >= edge, 2, 0)
    return (place == col).astype(F32).astype(BF)


def pack_kernel(
    tower_hbm, upper_hbm, lower_hbm, pre_upper_hbm, pre_lower_hbm, out_ref, lower_out_ref,
    tower_ref, upper_ref, lower_ref, pre_upper_ref, pre_lower_ref, weight_ref, tower_rows_ref, buf_ref, sem, in_sem,
):
    pieces = [(upper_hbm, upper_ref), (lower_hbm, lower_ref), (tower_hbm, tower_ref)]
    for source, target in ((pre_upper_hbm, pre_upper_ref), (pre_lower_hbm, pre_lower_ref)):
        pieces.append((source.at[:, pl.ds(source.shape[1] - 128, 128)], target.at[0]))
        pieces.append((source.at[:, pl.ds(0, 128)], target.at[1]))
    copies = [pltpu.make_async_copy(source, target, in_sem.at[i]) for i, (source, target) in enumerate(pieces)]
    for copy in copies:
        copy.start()
    for copy in copies[:1] + copies[2:]:
        copy.wait()
    weight_ref[...] = jnp.zeros((48, 512), F32)
    weight_ref[0:22, :] = sum(mm(upper_ref[k], one_hot(96, 96 * k, False)) for k in range(KWIDTH))
    last, first = (pre_upper_ref[i].astype(F32).T for i in range(2))
    low_last, low_first = (pre_lower_ref[i].astype(F32).T for i in range(2))
    weight_ref[22:24, 0:96] = last[126:128]
    weight_ref[23:24, 128:224] = last[125:126]
    weight_ref[22:24, 256:344] = low_last[126:128]
    tower_rows_ref[...] = jnp.zeros((128, 512), F32)
    for p in range(16):
        tower_rows_ref[8 * p + 6 : 8 * p + 8, 0:96] = first[0:2]
        tower_rows_ref[8 * p + 6 : 8 * p + 7, 128:224] = first[2:3]
        tower_rows_ref[8 * p + 6 : 8 * p + 8, 256:344] = low_first[0:2]
    weight = weight_ref[0:24, :].astype(BF)
    tower = tower_ref[...].astype(F32)
    for p in range(16):
        at, row = 512 * p, 8 * p
        tower_rows_ref[row : row + 3, :] = tower[:, at : at + 512]
        if p > 0:
            tower_rows_ref[row + 3 : row + 6, 0:128] = tower[:, at - 128 : at]
        tower_rows_ref[row + 3 : row + 6, 128:256] = tower[:, at + 256 : at + 384]
        tower_rows_ref[row + 3 : row + 6, 256:384] = tower[:, at + 128 : at + 256]
        if p < 15:
            tower_rows_ref[row + 3 : row + 6, 384:512] = tower[:, at + 512 : at + 640]
        buf_ref[p, 0:24, :] = weight
        buf_ref[p, 24:32, :] = tower_rows_ref[row : row + 8, :].astype(BF)
        pltpu.make_async_copy(buf_ref.at[p], out_ref.at[p], sem.at[p]).start()
    copies[1].wait()
    weight_ref[24:44, :] = sum(mm(lower_ref[k], one_hot(88, 96 * k, True)) for k in range(KWIDTH))
    lower_out_ref[...] = weight_ref[24:48, :].astype(BF)
    for p in range(16):
        pltpu.make_async_copy(buf_ref.at[p], out_ref.at[p], sem.at[p]).wait()


def edge_tiles(pos_ref, other_ref, at, deep):
    chip = pos_ref[0] * NY + pos_ref[1]
    before = other_ref[jnp.maximum(chip - 1 + pos_ref[2], 0), 16:24, :].astype(F32)
    after = other_ref[jnp.minimum(chip + pos_ref[2], NZ * NY - 1), 24:32, :].astype(F32)
    row = lax.broadcasted_iota(jnp.int32, (8, 128), 0)
    low = before[:, at : at + 128]
    high = pltpu.roll(after[:, at : at + 128], 2, 0)
    if deep:
        low = jnp.where(row == 5, pltpu.roll(before[:, at + 128 : at + 256], 6, 0), low)
        high = jnp.where(row == 2, pltpu.roll(after[:, at + 128 : at + 256], 4, 0), high)
    rest = jnp.zeros((120, 128), F32)
    return jnp.concatenate([rest, low], axis=0).T, jnp.concatenate([high, rest], axis=0).T


def upper_kernel(
    pos_ref, slope_ref, own_ref, other_ref, mid_ref, taps_out_ref, edge_out_ref,
    main_ref, edge_ref, w_ref, halo_ref, buf_ref, taps_ref, edge_rows_ref, sem,
):
    first = pos_ref[2] == 0
    for p in range(16):
        own, other = own_ref[p, 24:32, :].astype(F32), other_ref[p, 24:32, :].astype(F32)
        for j in range(2):
            rows = jnp.where(first, own, other) if j == 0 else jnp.where(first, other, own)
            rows = jnp.where(first, rows[:, 0:256], rows[:, 256:512])
            at = 3 * (2 * p + j)
            main_ref[at : at + 3, :] = rows[0:3]
            edge_ref[at : at + 3, :] = rows[3:6]
        own, other = own_ref[p, 0:24, :].astype(F32), other_ref[p, 0:24, :].astype(F32)
        both = [jnp.where(first, own, other), jnp.where(first, other, own)]
        w_ref[48 * p : 48 * p + 48, :] = jnp.concatenate(both, axis=0).astype(BF)
    spread = doubling()
    main = main_ref[...].astype(BF)
    edge = edge_ref[...].astype(BF)
    grad = jnp.concatenate(
        [
            mm(edge[:, :128], spread)[:, 128:],
            mm(main[:, :128], spread),
            mm(main[:, 128:], spread),
            mm(edge[:, 128:], spread)[:, :128],
        ],
        axis=1,
    )
    low, high = edge_tiles(pos_ref, other_ref, 0, True)
    slope = jnp.concatenate([half_slope(low[0:96]), slope_ref[...], half_slope(high[0:96])], axis=1)
    grad = grad * slope
    lane = lax.broadcasted_iota(jnp.int32, (96, 128), 1)
    taps_ref[480:512, :] = jnp.zeros((32, 512), BF)
    halo_ref[480:512, :] = jnp.zeros((32, 128), F32)
    for k in range(KWIDTH):
        moved = pltpu.roll(grad, 768 - (130 - k), 1)
        after = pltpu.roll(moved[:, 512:640], 126, 1)
        taps_ref[96 * k : 96 * k + 96, :] = moved[:, 0:512].astype(BF)
        halo_ref[96 * k : 96 * k + 96, :] = jnp.where(lane == 127, moved[:, 640:768], after)
    out_copies = [
        pltpu.make_async_copy(taps_ref, taps_out_ref, sem.at[2]),
        pltpu.make_async_copy(edge_rows_ref, edge_out_ref, sem.at[3]),
    ]
    out_copies[0].start()
    outside = lax.dot_general(
        halo_ref[...].T.astype(BF), w_ref[...], (((1,), (1,)), ((), ())), preferred_element_type=F32
    )[120:128]
    row = lax.broadcasted_iota(jnp.int32, (8, 256), 0)
    for half in range(2):
        lanes = slice(256 * half, 256 * half + 256)
        mid = mm(w_ref[...], taps_ref[:, lanes])
        for d in range(8):
            part = mid[96 * d : 96 * d + 96]
            if half == 0:
                moved = pltpu.roll(outside, (768 - 96 * d) % 768, 1)[:, 0:256]
                part = jnp.concatenate([part[0:16], jnp.where(row >= 6, moved, part[16:24]), part[24:]], axis=0)
            buf_ref[d, :, lanes] = part.astype(BF)
        out_copies.append(pltpu.make_async_copy(buf_ref.at[:, :, lanes], mid_ref.at[:, :, lanes], sem.at[half]))
        out_copies[-1].start()
    edge_rows_ref[...] = jnp.zeros((96, 256), F32)
    for half, tile in enumerate(edge_tiles(pos_ref, other_ref, 256, False)):
        for group in range(4):
            rows, lanes = slice(24 * group, 24 * group + 22), slice(128 * half, 128 * half + 128)
            edge_rows_ref[rows, lanes] = tile[22 * group : 22 * group + 22]
    out_copies[1].start()
    for copy in out_copies:
        copy.wait()


def lower_weight_kernel(pos_ref, own_ref, other_ref, out_ref, rows_ref):
    first = pos_ref[2] == 0
    for p in range(16):
        slot = lax.rem(pos_ref[1] - p % NY + NY, NY) * NZ + lax.rem(pos_ref[0] - p // NY + NZ, NZ)
        own, other = own_ref[slot].astype(F32), other_ref[slot].astype(F32)
        rows_ref[40 * p : 40 * p + 24, :] = jnp.where(first, own, other)
        rows_ref[40 * p + 20 : 40 * p + 44, :] = jnp.where(first, other, own)
    out_ref[...] = rows_ref[0:640, :].astype(BF)


def lower_taps_kernel(pos_ref, mid_ref, slope_copy, slope_ref, edge_ref, taps_ref):
    place = pos_ref[0] * (NY * NC) + pos_ref[1] * NC + pos_ref[2]
    total = mid_ref[0].astype(F32)
    for d in range(1, 8):
        total = total + mid_ref[d].astype(F32)
    mid = total.astype(BF)
    ends = mid[:, 0:128].astype(F32).T
    left = jnp.broadcast_to(jnp.where(place == 0, 0.0, ends[0:96, 23:24]), (96, 128))
    right = jnp.broadcast_to(jnp.where(place == 31, 0.0, ends[0:96, 22:23]), (96, 128))
    edge = half_slope(edge_ref[...])
    spread = doubling()
    grad = jnp.concatenate([mm(mid[:, 128 * j : 128 * j + 128], spread) for j in range(4)], axis=1)
    slope_copy.wait()
    grad = jnp.concatenate(
        [left * edge[:, 0:128], grad * slope_ref[...], right * edge[:, 128:256]], axis=1
    )
    taps_ref[480:512, :] = jnp.zeros((32, 1024), BF)
    for k in range(KWIDTH):
        moved = pltpu.roll(grad, 1280 - (130 - k), 1)
        taps_ref[96 * k : 96 * k + 96, :] = moved[:, 0:1024].astype(BF)


def low_kernel(taps_ref, w_ref, low_ref, buf_ref, sem):
    for quarter in range(4):
        lanes = slice(256 * quarter, 256 * quarter + 256)
        low = mm(w_ref[...], taps_ref[:, lanes])
        for d in range(8):
            buf_ref[d, :, lanes] = low[80 * d : 80 * d + 80].astype(BF)
        pltpu.make_async_copy(buf_ref.at[:, :, lanes], low_ref.at[:, :, lanes], sem.at[quarter]).start()
    for quarter in range(4):
        lanes = slice(256 * quarter, 256 * quarter + 256)
        pltpu.make_async_copy(buf_ref.at[:, :, lanes], low_ref.at[:, :, lanes], sem.at[quarter]).wait()


def total_kernel(low_ref, out_ref):
    total = low_ref[0].astype(F32)
    for d in range(1, 8):
        total = total + low_ref[d].astype(F32)
    out_ref[...] = total.astype(BF)


def fetched_weight_grad_kernel(
    pos_ref, act_hbm, taps_hbm, keep_ref, send_ref, rows_ref, block_ref, act_ref, taps_ref, sem
):
    copies = [
        pltpu.make_async_copy(act_hbm, act_ref, sem.at[0]),
        pltpu.make_async_copy(taps_hbm, taps_ref, sem.at[1]),
    ]
    for copy in copies:
        copy.start()
    for copy in copies:
        copy.wait()
    weight_grad_kernel(pos_ref, act_ref, taps_ref, keep_ref, send_ref, rows_ref, block_ref)


def weight_grad_kernel(pos_ref, act_ref, taps_ref, keep_ref, send_ref, rows_ref, block_ref):
    channels, count = act_ref.shape
    width = channels // 32
    rows_ref[channels:, :] = jnp.zeros((8, rows_ref.shape[1]), F32)
    rows_ref[0:channels, :] = lax.dot_general(
        act_ref[...], taps_ref[:, 0:count], (((1,), (1,)), ((), ())), preferred_element_type=F32
    )
    for q in range(32):
        block_ref[q] = rows_ref[width * q : width * q + 24, :]
    for ry in range(NY):
        for rz in range(NZ):
            zh = lax.rem(pos_ref[0] + rz, NZ)
            y = lax.rem(pos_ref[1] + ry, NY)
            base = (zh * NY + y) * NC
            keep_ref[ry, rz] = block_ref[base + pos_ref[2]]
            send_ref[ry, rz] = block_ref[base + 1 - pos_ref[2]].astype(BF)


def lower_kernel(
    pos_ref, mid_ref, slope_hbm, edge_ref, act_hbm, taps_ref, keep_ref, send_ref,
    rows_ref, block_ref, slope_ref, act_ref, sem,
):
    copies = [
        pltpu.make_async_copy(slope_hbm, slope_ref, sem.at[0]),
        pltpu.make_async_copy(act_hbm, act_ref, sem.at[1]),
    ]
    for copy in copies:
        copy.start()
    lower_taps_kernel(pos_ref, mid_ref, copies[0], slope_ref, edge_ref, taps_ref)
    copies[1].wait()
    weight_grad_kernel(pos_ref, act_ref, taps_ref, keep_ref, send_ref, rows_ref, block_ref)


def weight_grad(pos, act, taps, fetch):
    block = (NY, NZ, 24, taps.shape[0])
    scratch = [pltpu.VMEM((act.shape[0] + 8, taps.shape[0]), F32), pltpu.VMEM((32, 24, taps.shape[0]), F32)]
    if fetch:
        scratch += [pltpu.VMEM(act.shape, BF), pltpu.VMEM(taps.shape, BF), pltpu.SemaphoreType.DMA((2,))]
        act, taps = (pltpu.with_memory_space_constraint(v, pltpu.HBM) for v in (act, taps))
    return pl.pallas_call(
        fetched_weight_grad_kernel if fetch else weight_grad_kernel,
        out_shape=(jax.ShapeDtypeStruct(block, F32), jax.ShapeDtypeStruct(block, BF)),
        in_specs=[SMEM] + [HBM if fetch else VMEM] * 2,
        out_specs=(VMEM, VMEM),
        scratch_shapes=scratch,
        compiler_params=PARAMS,
        name="weight_grad",
    )(pos, act, taps)


def local(tower_grad, act_mid, pre_mid, act_low, pre_low, weight_upper, weight_lower):
    pos = jnp.stack([lax.axis_index("zh"), lax.axis_index("y"), lax.axis_index("c")]).astype(jnp.int32)
    sources = (tower_grad.T, weight_upper, weight_lower, pre_mid.T, pre_low.T)
    packed, lower_block = pl.pallas_call(
        pack_kernel,
        out_shape=(pltpu.HBM((16, 32, 512), BF), jax.ShapeDtypeStruct((24, 512), BF)),
        in_specs=[HBM] * 5,
        out_specs=(HBM, VMEM),
        scratch_shapes=[
            pltpu.VMEM((3, 8192), BF),
            pltpu.VMEM(weight_upper.shape, BF),
            pltpu.VMEM(weight_lower.shape, BF),
            pltpu.VMEM((2, 96, 128), BF),
            pltpu.VMEM((2, 88, 128), BF),
            pltpu.VMEM((48, 512), F32),
            pltpu.VMEM((128, 512), F32),
            pltpu.VMEM((16, 32, 512), BF),
            pltpu.SemaphoreType.DMA((16,)),
            pltpu.SemaphoreType.DMA((7,)),
        ],
        compiler_params=PARAMS,
        name="pack",
    )(*(pltpu.with_memory_space_constraint(v, pltpu.HBM) for v in sources))
    pre_lower = jnp.pad(pre_low.T.reshape(4, 22, 1024), ((0, 0), (0, 2), (0, 0))).reshape(96, 1024)
    slope_upper = half_slope(pre_mid.T)
    slope_lower = half_slope(pre_lower)
    act_low_rows = act_low.T
    lower_blocks = [lower_block] + [shifted(lower_block, "zh", NZ, s) for s in range(1, NZ)]
    own = lax.all_to_all(packed, ("zh", "y"), split_axis=0, concat_axis=0, tiled=True)
    own, slope_upper, slope_lower, act_low_rows, lower_blocks = lax.optimization_barrier(
        (own, slope_upper, slope_lower, act_low_rows, lower_blocks)
    )
    other = shifted(own, "c", NC, 1)

    mid_part, upper_taps, edges = pl.pallas_call(
        upper_kernel,
        out_shape=(pltpu.HBM((8, 96, 512), BF), pltpu.HBM((512, 512), BF), pltpu.HBM((96, 256), F32)),
        in_specs=[SMEM] + [VMEM] * 3,
        out_specs=(HBM, HBM, HBM),
        scratch_shapes=[
            pltpu.VMEM((96, 256), F32),
            pltpu.VMEM((96, 256), F32),
            pltpu.VMEM((768, 512), BF),
            pltpu.VMEM((512, 128), F32),
            pltpu.VMEM((8, 96, 512), BF),
            pltpu.VMEM((512, 512), BF),
            pltpu.VMEM((96, 256), F32),
            pltpu.SemaphoreType.DMA((4,)),
        ],
        compiler_params=PARAMS,
        name="upper",
    )(pos, slope_upper, own, other)
    mid_parts = lax.all_to_all(mid_part, DP, split_axis=0, concat_axis=0, tiled=True)

    lower_blocks, _ = lax.optimization_barrier((lower_blocks, upper_taps))
    lower_level = jnp.stack(lower_blocks)
    lower_levels = [lower_level] + [shifted(lower_level, "y", NY, s) for s in range(1, NY)]
    upper_keep, upper_send = weight_grad(pos, act_mid.T, upper_taps, True)
    lower_levels, upper_send = lax.optimization_barrier((lower_levels, upper_send))
    lower_own = join(lower_levels)
    lower_own, upper_send = lax.optimization_barrier((lower_own, upper_send))
    upper_got = shifted(upper_send, "c", NC, 1)
    lower_other = shifted(lower_own, "c", NC, 1)
    lower_full = pl.pallas_call(
        lower_weight_kernel,
        out_shape=jax.ShapeDtypeStruct((640, 512), BF),
        in_specs=[SMEM] + [VMEM] * 2,
        out_specs=VMEM,
        scratch_shapes=[pltpu.VMEM((648, 512), F32)],
        compiler_params=PARAMS,
        name="lower_weight",
    )(pos, lower_own, lower_other)

    mid_parts, upper_got = lax.optimization_barrier((mid_parts, upper_got))
    block = (NY, NZ, 24, 512)
    fetched = [pltpu.with_memory_space_constraint(v, pltpu.HBM) for v in (slope_lower, act_low_rows)]
    lower_taps, lower_keep, lower_send = pl.pallas_call(
        lower_kernel,
        out_shape=(
            jax.ShapeDtypeStruct((512, 1024), BF),
            jax.ShapeDtypeStruct(block, F32),
            jax.ShapeDtypeStruct(block, BF),
        ),
        in_specs=[SMEM, VMEM, HBM, VMEM, HBM],
        out_specs=(VMEM, VMEM, VMEM),
        scratch_shapes=[
            pltpu.VMEM((act_low_rows.shape[0] + 8, 512), F32),
            pltpu.VMEM((32, 24, 512), F32),
            pltpu.VMEM(slope_lower.shape, F32),
            pltpu.VMEM(act_low_rows.shape, BF),
            pltpu.SemaphoreType.DMA((2,)),
        ],
        compiler_params=PARAMS,
        name="lower",
    )(pos, mid_parts, fetched[0], edges, fetched[1])
    lower_got = shifted(lower_send, "c", NC, 1)
    own_sum, *sends = core_sum((upper_keep, upper_got), (lower_keep, lower_got))
    lower_taps, _ = lax.optimization_barrier((lower_taps, lower_keep))
    low_part = pl.pallas_call(
        low_kernel,
        out_shape=pltpu.HBM((8, 80, 1024), BF),
        in_specs=[VMEM] * 2,
        out_specs=HBM,
        scratch_shapes=[pltpu.VMEM((8, 80, 1024), BF), pltpu.SemaphoreType.DMA((4,))],
        compiler_params=PARAMS,
        name="low",
    )(lower_taps, lower_full)
    low_part, _ = lax.optimization_barrier((low_part, lower_got))
    low_parts = lax.all_to_all(low_part, DP, split_axis=0, concat_axis=0, tiled=True)
    got = [shifted(send, "y", NY, s + 1) for s, send in enumerate(sends)]
    low_grad = pl.pallas_call(
        total_kernel,
        out_shape=jax.ShapeDtypeStruct((80, 1024), BF),
        in_specs=[VMEM],
        out_specs=VMEM,
        compiler_params=PARAMS,
        name="low_total",
    )(low_parts)
    scales = tuple(1.0 / math.sqrt(act.shape[0] * NZ * NY * NC) for act in (act_mid, act_low))
    low_grad, grad_upper, grad_lower = z_sum(own_sum, got, low_grad, scales, weight_upper.shape, weight_lower.shape)
    return low_grad.T, grad_upper, grad_lower


def solution(mesh):
    fine = Mesh(mesh.devices.reshape(4, 2, NZ, NY, NC), DP + SEQ)
    in_specs = (
        P(None, DP + SEQ),
        P(SEQ, None),
        P(SEQ, DP),
        P(SEQ, None),
        P(SEQ, DP),
        P(None, SEQ, DP),
        P(None, SEQ, DP),
    )
    out_specs = (P(SEQ, DP), P(None, SEQ, DP), P(None, SEQ, DP))
    return jax.shard_map(local, mesh=fine, in_specs=in_specs, out_specs=out_specs, check_vma=False)
```

```python
import functools
import math

import jax
import jax.numpy as jnp
from jax import lax
from jax.experimental import pallas as pl
from jax.experimental.pallas import tpu as pltpu
from jax.sharding import Mesh, PartitionSpec as P

KWIDTH = 5
HALF = 2
DP = ("x", "zl")
SEQ = ("zh", "y", "c")
NZ, NY, NC = 4, 4, 2
BF = jnp.bfloat16
F32 = jnp.float32
PARAMS = pltpu.CompilerParams(vmem_limit_bytes=16 * 1024 * 1024)
VMEM = pl.BlockSpec(memory_space=pltpu.VMEM)
SMEM = pl.BlockSpec(memory_space=pltpu.SMEM)
HBM = pl.BlockSpec(memory_space=pltpu.HBM)


def half_slope(pre_act):
    values = pre_act.astype(F32)
    cumulative = 0.5 * (1.0 + lax.erf(values * (1.0 / math.sqrt(2.0))))
    density = jnp.exp(-0.5 * values * values) * (1.0 / math.sqrt(2.0 * math.pi))
    return 0.5 * (cumulative + values * density)


def shifted(block, axis, count, step):
    return lax.ppermute(block, axis, [(i, (i + step) % count) for i in range(count)])


def join_kernel(*refs):
    out_ref = refs[-1]
    for s in range(NY):
        out_ref[NZ * s : NZ * s + NZ] = refs[s][...]


def join(levels):
    shape = (NY * NZ,) + levels[0].shape[1:]
    return pl.pallas_call(
        join_kernel,
        out_shape=jax.ShapeDtypeStruct(shape, BF),
        in_specs=[VMEM] * NY,
        out_specs=VMEM,
        compiler_params=PARAMS,
        name="join",
    )(*levels)


def core_sum_kernel(keep_upper_ref, got_upper_hbm, keep_lower_ref, got_lower_ref, own_ref, *refs):
    send_refs, (got_upper_ref, sem) = refs[: NY - 1], refs[NY - 1 :]
    fetch = pltpu.make_async_copy(got_upper_hbm, got_upper_ref, sem)
    fetch.start()
    for half, (keep_ref, got_ref) in ((1, (keep_lower_ref, got_lower_ref)), (0, (keep_upper_ref, got_upper_ref))):
        if half == 0:
            fetch.wait()
        rows = slice(24 * half, 24 * half + 24)
        for s in range(NY):
            for z in range(NZ):
                total = keep_ref[s, z] + got_ref[s, z].astype(F32)
                if s == 0:
                    own_ref[z, rows] = total
                else:
                    send_refs[s - 1][z, rows] = total.astype(BF)


def y_sum_kernel(own_ref, *refs):
    got_refs, total_ref, send_refs = refs[: NY - 1], refs[NY - 1], refs[NY:]
    for z in range(NZ):
        total = own_ref[z]
        for got_ref in got_refs:
            total = total + got_ref[z].astype(F32)
        if z == 0:
            total_ref[...] = total
        else:
            send_refs[z - 1][...] = total.astype(BF)


def z_sum_kernel(scales, own_ref, *refs):
    got_refs, upper_ref, lower_ref = refs[: NZ - 1], refs[NZ - 1], refs[NZ]
    total = own_ref[...]
    for got_ref in got_refs:
        total = total + got_ref[...].astype(F32)
    lane = lax.broadcasted_iota(jnp.int32, (24, 512), 1)
    for k in range(KWIDTH):
        upper_ref[k] = pltpu.roll(total[0:24], (512 - 96 * k) % 512, 1)[0:22, 0:96] * scales[0]
        lower = pltpu.roll(total[24:48], (512 - 96 * k) % 512, 1)
        packed = lower
        for group in range(1, 4):
            packed = jnp.where(lane >= 22 * group, pltpu.roll(lower, 512 - 2 * group, 1), packed)
        lower_ref[k] = packed[0:20, 0:88] * scales[1]


def small_call(kernel, name, out_shape, *operands):
    return pl.pallas_call(
        kernel,
        out_shape=out_shape,
        in_specs=[VMEM] * len(operands),
        out_specs=tuple(VMEM for _ in out_shape),
        compiler_params=PARAMS,
        name=name,
    )(*operands)


def core_sum(upper, lower):
    level = jax.ShapeDtypeStruct((NZ, 48, 512), BF)
    outs = (jax.ShapeDtypeStruct(level.shape, F32),) + (level,) * (NY - 1)
    got_upper = pltpu.with_memory_space_constraint(upper[1], pltpu.HBM)
    return pl.pallas_call(
        core_sum_kernel,
        out_shape=outs,
        in_specs=[VMEM, HBM, VMEM, VMEM],
        out_specs=tuple(VMEM for _ in outs),
        scratch_shapes=[pltpu.VMEM(got_upper.shape, BF), pltpu.SemaphoreType.DMA(())],
        compiler_params=PARAMS,
        name="core_sum",
    )(upper[0], got_upper, *lower)


def z_sum(own, got, low_grad, scales, upper_shape, lower_shape):
    block = jax.ShapeDtypeStruct((48, 512), BF)
    own, *sends = small_call(
        y_sum_kernel, "y_sum", (jax.ShapeDtypeStruct(block.shape, F32),) + (block,) * (NZ - 1), own, *got
    )
    got = [shifted(send, "zh", NZ, s + 1) for s, send in enumerate(sends)]
    got, low_grad = lax.optimization_barrier((got, low_grad))
    outs = (jax.ShapeDtypeStruct(upper_shape, F32), jax.ShapeDtypeStruct(lower_shape, F32))
    return low_grad, *small_call(functools.partial(z_sum_kernel, scales), "z_sum", outs, own, *got)


def doubling():
    row = lax.broadcasted_iota(jnp.int32, (128, 256), 0)
    col = lax.broadcasted_iota(jnp.int32, (128, 256), 1)
    return (row == lax.shift_right_logical(col, 1)).astype(F32).astype(BF)


def mm(a, b):
    return jnp.dot(a, b, preferred_element_type=F32)


def one_hot(rows, start, pads):
    row = lax.broadcasted_iota(jnp.int32, (rows, 512), 0)
    col = lax.broadcasted_iota(jnp.int32, (rows, 512), 1)
    place = row + start
    if pads:
        for edge in (22, 44, 66):
            place = place + jnp.where(row >= edge, 2, 0)
    return (place == col).astype(F32).astype(BF)


def pack_kernel(
    tower_hbm, upper_hbm, lower_hbm, pre_upper_hbm, pre_lower_hbm, out_ref, lower_out_ref,
    tower_ref, upper_ref, lower_ref, pre_upper_ref, pre_lower_ref, weight_ref, tower_rows_ref, buf_ref, sem, in_sem,
):
    pieces = [(upper_hbm, upper_ref), (lower_hbm, lower_ref), (tower_hbm, tower_ref)]
    for source, target in ((pre_upper_hbm, pre_upper_ref), (pre_lower_hbm, pre_lower_ref)):
        pieces.append((source.at[:, pl.ds(source.shape[1] - 128, 128)], target.at[0]))
        pieces.append((source.at[:, pl.ds(0, 128)], target.at[1]))
    copies = [pltpu.make_async_copy(source, target, in_sem.at[i]) for i, (source, target) in enumerate(pieces)]
    for copy in copies:
        copy.start()
    for copy in copies[:1] + copies[2:]:
        copy.wait()
    weight_ref[...] = jnp.zeros((48, 512), F32)
    weight_ref[0:22, :] = sum(mm(upper_ref[k], one_hot(96, 96 * k, False)) for k in range(KWIDTH))
    last, first = (pre_upper_ref[i].astype(F32).T for i in range(2))
    low_last, low_first = (pre_lower_ref[i].astype(F32).T for i in range(2))
    weight_ref[22:24, 0:96] = last[126:128]
    weight_ref[23:24, 128:224] = last[125:126]
    weight_ref[22:24, 256:344] = low_last[126:128]
    tower_rows_ref[...] = jnp.zeros((128, 512), F32)
    for p in range(16):
        tower_rows_ref[8 * p + 6 : 8 * p + 8, 0:96] = first[0:2]
        tower_rows_ref[8 * p + 6 : 8 * p + 7, 128:224] = first[2:3]
        tower_rows_ref[8 * p + 6 : 8 * p + 8, 256:344] = low_first[0:2]
    weight = weight_ref[0:24, :].astype(BF)
    tower = tower_ref[...].astype(F32)
    for p in range(16):
        at, row = 512 * p, 8 * p
        tower_rows_ref[row : row + 3, :] = tower[:, at : at + 512]
        if p > 0:
            tower_rows_ref[row + 3 : row + 6, 0:128] = tower[:, at - 128 : at]
        tower_rows_ref[row + 3 : row + 6, 128:256] = tower[:, at + 256 : at + 384]
        tower_rows_ref[row + 3 : row + 6, 256:384] = tower[:, at + 128 : at + 256]
        if p < 15:
            tower_rows_ref[row + 3 : row + 6, 384:512] = tower[:, at + 512 : at + 640]
        buf_ref[p, 0:24, :] = weight
        buf_ref[p, 24:32, :] = tower_rows_ref[row : row + 8, :].astype(BF)
        pltpu.make_async_copy(buf_ref.at[p], out_ref.at[p], sem.at[p]).start()
    copies[1].wait()
    weight_ref[24:44, :] = sum(mm(lower_ref[k], one_hot(88, 96 * k, True)) for k in range(KWIDTH))
    lower_out_ref[...] = weight_ref[24:48, :].astype(BF)
    for p in range(16):
        pltpu.make_async_copy(buf_ref.at[p], out_ref.at[p], sem.at[p]).wait()


def edge_tiles(pos_ref, other_ref, at, deep):
    chip = pos_ref[0] * NY + pos_ref[1]
    before = other_ref[jnp.maximum(chip - 1 + pos_ref[2], 0), 16:24, :].astype(F32)
    after = other_ref[jnp.minimum(chip + pos_ref[2], NZ * NY - 1), 24:32, :].astype(F32)
    row = lax.broadcasted_iota(jnp.int32, (8, 128), 0)
    low = before[:, at : at + 128]
    high = pltpu.roll(after[:, at : at + 128], 2, 0)
    if deep:
        low = jnp.where(row == 5, pltpu.roll(before[:, at + 128 : at + 256], 6, 0), low)
        high = jnp.where(row == 2, pltpu.roll(after[:, at + 128 : at + 256], 4, 0), high)
    rest = jnp.zeros((120, 128), F32)
    return jnp.concatenate([rest, low], axis=0).T, jnp.concatenate([high, rest], axis=0).T


def upper_kernel(
    pos_ref, slope_ref, own_ref, other_ref, mid_ref, taps_out_ref, edge_out_ref,
    main_ref, edge_ref, w_ref, halo_ref, buf_ref, taps_ref, edge_rows_ref, sem,
):
    first = pos_ref[2] == 0
    for p in range(16):
        own, other = own_ref[p, 24:32, :].astype(F32), other_ref[p, 24:32, :].astype(F32)
        for j in range(2):
            rows = jnp.where(first, own, other) if j == 0 else jnp.where(first, other, own)
            rows = jnp.where(first, rows[:, 0:256], rows[:, 256:512])
            at = 3 * (2 * p + j)
            main_ref[at : at + 3, :] = rows[0:3]
            edge_ref[at : at + 3, :] = rows[3:6]
        own, other = own_ref[p, 0:24, :].astype(F32), other_ref[p, 0:24, :].astype(F32)
        both = [jnp.where(first, own, other), jnp.where(first, other, own)]
        w_ref[48 * p : 48 * p + 48, :] = jnp.concatenate(both, axis=0).astype(BF)
    spread = doubling()
    main = main_ref[...].astype(BF)
    edge = edge_ref[...].astype(BF)
    grad = jnp.concatenate(
        [
            mm(edge[:, :128], spread)[:, 128:],
            mm(main[:, :128], spread),
            mm(main[:, 128:], spread),
            mm(edge[:, 128:], spread)[:, :128],
        ],
        axis=1,
    )
    low, high = edge_tiles(pos_ref, other_ref, 0, True)
    slope = jnp.concatenate([half_slope(low[0:96]), slope_ref[...], half_slope(high[0:96])], axis=1)
    grad = grad * slope
    lane = lax.broadcasted_iota(jnp.int32, (96, 128), 1)
    taps_ref[480:512, :] = jnp.zeros((32, 512), BF)
    halo_ref[480:512, :] = jnp.zeros((32, 128), F32)
    for k in range(KWIDTH):
        moved = pltpu.roll(grad, 768 - (130 - k), 1)
        after = pltpu.roll(moved[:, 512:640], 126, 1)
        taps_ref[96 * k : 96 * k + 96, :] = moved[:, 0:512].astype(BF)
        halo_ref[96 * k : 96 * k + 96, :] = jnp.where(lane == 127, moved[:, 640:768], after)
    out_copies = [
        pltpu.make_async_copy(taps_ref, taps_out_ref, sem.at[2]),
        pltpu.make_async_copy(edge_rows_ref, edge_out_ref, sem.at[3]),
    ]
    out_copies[0].start()
    outside = lax.dot_general(
        halo_ref[...].T.astype(BF), w_ref[...], (((1,), (1,)), ((), ())), preferred_element_type=F32
    )[120:128]
    row = lax.broadcasted_iota(jnp.int32, (8, 256), 0)
    for half in range(2):
        lanes = slice(256 * half, 256 * half + 256)
        mid = mm(w_ref[...], taps_ref[:, lanes])
        for d in range(8):
            part = mid[96 * d : 96 * d + 96]
            if half == 0:
                moved = pltpu.roll(outside, (768 - 96 * d) % 768, 1)[:, 0:256]
                part = jnp.concatenate([part[0:16], jnp.where(row >= 6, moved, part[16:24]), part[24:]], axis=0)
            buf_ref[d, :, lanes] = part.astype(BF)
        out_copies.append(pltpu.make_async_copy(buf_ref.at[:, :, lanes], mid_ref.at[:, :, lanes], sem.at[half]))
        out_copies[-1].start()
    edge_rows_ref[...] = jnp.zeros((96, 256), F32)
    for half, tile in enumerate(edge_tiles(pos_ref, other_ref, 256, False)):
        for group in range(4):
            rows, lanes = slice(24 * group, 24 * group + 22), slice(128 * half, 128 * half + 128)
            edge_rows_ref[rows, lanes] = tile[22 * group : 22 * group + 22]
    out_copies[1].start()
    for copy in out_copies:
        copy.wait()


def lower_weight_kernel(pos_ref, own_ref, other_ref, out_ref, rows_ref):
    first = pos_ref[2] == 0
    for p in range(16):
        slot = lax.rem(pos_ref[1] - p % NY + NY, NY) * NZ + lax.rem(pos_ref[0] - p // NY + NZ, NZ)
        own, other = own_ref[slot].astype(F32), other_ref[slot].astype(F32)
        rows_ref[40 * p : 40 * p + 24, :] = jnp.where(first, own, other)
        rows_ref[40 * p + 20 : 40 * p + 44, :] = jnp.where(first, other, own)
    out_ref[...] = rows_ref[0:640, :].astype(BF)


def lower_taps_kernel(pos_ref, mid_ref, slope_ref, edge_ref, taps_ref):
    place = pos_ref[0] * (NY * NC) + pos_ref[1] * NC + pos_ref[2]
    total = mid_ref[0].astype(F32)
    for d in range(1, 8):
        total = total + mid_ref[d].astype(F32)
    mid = total.astype(BF)
    ends = mid[:, 0:128].astype(F32).T
    left = jnp.broadcast_to(jnp.where(place == 0, 0.0, ends[0:96, 23:24]), (96, 128))
    right = jnp.broadcast_to(jnp.where(place == 31, 0.0, ends[0:96, 22:23]), (96, 128))
    edge = half_slope(edge_ref[...])
    spread = doubling()
    grad = jnp.concatenate([mm(mid[:, 128 * j : 128 * j + 128], spread) for j in range(4)], axis=1)
    grad = jnp.concatenate(
        [left * edge[:, 0:128], grad * slope_ref[...], right * edge[:, 128:256]], axis=1
    )
    taps_ref[480:512, :] = jnp.zeros((32, 1024), BF)
    for k in range(KWIDTH):
        moved = pltpu.roll(grad, 1280 - (130 - k), 1)
        taps_ref[96 * k : 96 * k + 96, :] = moved[:, 0:1024].astype(BF)


def low_kernel(taps_ref, w_ref, low_ref, buf_ref, sem):
    for quarter in range(4):
        lanes = slice(256 * quarter, 256 * quarter + 256)
        low = mm(w_ref[...], taps_ref[:, lanes])
        for d in range(8):
            buf_ref[d, :, lanes] = low[80 * d : 80 * d + 80].astype(BF)
        pltpu.make_async_copy(buf_ref.at[:, :, lanes], low_ref.at[:, :, lanes], sem.at[quarter]).start()
    for quarter in range(4):
        lanes = slice(256 * quarter, 256 * quarter + 256)
        pltpu.make_async_copy(buf_ref.at[:, :, lanes], low_ref.at[:, :, lanes], sem.at[quarter]).wait()


def total_kernel(low_ref, out_ref):
    total = low_ref[0].astype(F32)
    for d in range(1, 8):
        total = total + low_ref[d].astype(F32)
    out_ref[...] = total.astype(BF)


def fetched_weight_grad_kernel(
    pos_ref, act_hbm, taps_hbm, keep_ref, send_ref, rows_ref, block_ref, act_ref, taps_ref, sem
):
    copies = [
        pltpu.make_async_copy(act_hbm, act_ref, sem.at[0]),
        pltpu.make_async_copy(taps_hbm, taps_ref, sem.at[1]),
    ]
    for copy in copies:
        copy.start()
    for copy in copies:
        copy.wait()
    weight_grad_kernel(pos_ref, act_ref, taps_ref, keep_ref, send_ref, rows_ref, block_ref)


def weight_grad_kernel(pos_ref, act_ref, taps_ref, keep_ref, send_ref, rows_ref, block_ref):
    channels, count = act_ref.shape
    width = channels // 32
    rows_ref[channels:, :] = jnp.zeros((8, rows_ref.shape[1]), F32)
    rows_ref[0:channels, :] = lax.dot_general(
        act_ref[...], taps_ref[:, 0:count], (((1,), (1,)), ((), ())), preferred_element_type=F32
    )
    for q in range(32):
        block_ref[q] = rows_ref[width * q : width * q + 24, :]
    for ry in range(NY):
        for rz in range(NZ):
            zh = lax.rem(pos_ref[0] + rz, NZ)
            y = lax.rem(pos_ref[1] + ry, NY)
            base = (zh * NY + y) * NC
            keep_ref[ry, rz] = block_ref[base + pos_ref[2]]
            send_ref[ry, rz] = block_ref[base + 1 - pos_ref[2]].astype(BF)


def weight_grad(pos, act, taps, fetch):
    block = (NY, NZ, 24, taps.shape[0])
    scratch = [pltpu.VMEM((act.shape[0] + 8, taps.shape[0]), F32), pltpu.VMEM((32, 24, taps.shape[0]), F32)]
    if fetch:
        scratch += [pltpu.VMEM(act.shape, BF), pltpu.VMEM(taps.shape, BF), pltpu.SemaphoreType.DMA((2,))]
        act, taps = (pltpu.with_memory_space_constraint(v, pltpu.HBM) for v in (act, taps))
    return pl.pallas_call(
        fetched_weight_grad_kernel if fetch else weight_grad_kernel,
        out_shape=(jax.ShapeDtypeStruct(block, F32), jax.ShapeDtypeStruct(block, BF)),
        in_specs=[SMEM] + [HBM if fetch else VMEM] * 2,
        out_specs=(VMEM, VMEM),
        scratch_shapes=scratch,
        compiler_params=PARAMS,
        name="weight_grad",
    )(pos, act, taps)


def local(tower_grad, act_mid, pre_mid, act_low, pre_low, weight_upper, weight_lower):
    pos = jnp.stack([lax.axis_index("zh"), lax.axis_index("y"), lax.axis_index("c")]).astype(jnp.int32)
    sources = (tower_grad.T, weight_upper, weight_lower, pre_mid.T, pre_low.T)
    packed, lower_block = pl.pallas_call(
        pack_kernel,
        out_shape=(pltpu.HBM((16, 32, 512), BF), jax.ShapeDtypeStruct((24, 512), BF)),
        in_specs=[HBM] * 5,
        out_specs=(HBM, VMEM),
        scratch_shapes=[
            pltpu.VMEM((3, 8192), BF),
            pltpu.VMEM(weight_upper.shape, BF),
            pltpu.VMEM(weight_lower.shape, BF),
            pltpu.VMEM((2, 96, 128), BF),
            pltpu.VMEM((2, 88, 128), BF),
            pltpu.VMEM((48, 512), F32),
            pltpu.VMEM((128, 512), F32),
            pltpu.VMEM((16, 32, 512), BF),
            pltpu.SemaphoreType.DMA((16,)),
            pltpu.SemaphoreType.DMA((7,)),
        ],
        compiler_params=PARAMS,
        name="pack",
    )(*(pltpu.with_memory_space_constraint(v, pltpu.HBM) for v in sources))
    pre_lower = jnp.pad(pre_low.T.reshape(4, 22, 1024), ((0, 0), (0, 2), (0, 0))).reshape(96, 1024)
    slope_upper = half_slope(pre_mid.T)
    slope_lower = half_slope(pre_lower)
    act_low_rows = act_low.T
    lower_blocks = [lower_block] + [shifted(lower_block, "zh", NZ, s) for s in range(1, NZ)]
    own = lax.all_to_all(packed, ("zh", "y"), split_axis=0, concat_axis=0, tiled=True)
    own, slope_upper, slope_lower, act_low_rows, lower_blocks = lax.optimization_barrier(
        (own, slope_upper, slope_lower, act_low_rows, lower_blocks)
    )
    other = shifted(own, "c", NC, 1)

    mid_part, upper_taps, edges = pl.pallas_call(
        upper_kernel,
        out_shape=(pltpu.HBM((8, 96, 512), BF), pltpu.HBM((512, 512), BF), pltpu.HBM((96, 256), F32)),
        in_specs=[SMEM] + [VMEM] * 3,
        out_specs=(HBM, HBM, HBM),
        scratch_shapes=[
            pltpu.VMEM((96, 256), F32),
            pltpu.VMEM((96, 256), F32),
            pltpu.VMEM((768, 512), BF),
            pltpu.VMEM((512, 128), F32),
            pltpu.VMEM((8, 96, 512), BF),
            pltpu.VMEM((512, 512), BF),
            pltpu.VMEM((96, 256), F32),
            pltpu.SemaphoreType.DMA((4,)),
        ],
        compiler_params=PARAMS,
        name="upper",
    )(pos, slope_upper, own, other)
    mid_parts = lax.all_to_all(mid_part, DP, split_axis=0, concat_axis=0, tiled=True)

    lower_blocks, _ = lax.optimization_barrier((lower_blocks, upper_taps))
    lower_level = jnp.stack(lower_blocks)
    lower_levels = [lower_level] + [shifted(lower_level, "y", NY, s) for s in range(1, NY)]
    upper_keep, upper_send = weight_grad(pos, act_mid.T, upper_taps, True)
    lower_levels, upper_send = lax.optimization_barrier((lower_levels, upper_send))
    lower_own = join(lower_levels)
    lower_own, upper_send = lax.optimization_barrier((lower_own, upper_send))
    upper_got = shifted(upper_send, "c", NC, 1)
    lower_other = shifted(lower_own, "c", NC, 1)
    lower_full = pl.pallas_call(
        lower_weight_kernel,
        out_shape=jax.ShapeDtypeStruct((640, 512), BF),
        in_specs=[SMEM] + [VMEM] * 2,
        out_specs=VMEM,
        scratch_shapes=[pltpu.VMEM((648, 512), F32)],
        compiler_params=PARAMS,
        name="lower_weight",
    )(pos, lower_own, lower_other)

    mid_parts, upper_got = lax.optimization_barrier((mid_parts, upper_got))
    lower_taps = pl.pallas_call(
        lower_taps_kernel,
        out_shape=jax.ShapeDtypeStruct((512, 1024), BF),
        in_specs=[SMEM] + [VMEM] * 3,
        out_specs=VMEM,
        compiler_params=PARAMS,
        name="lower_taps",
    )(pos, mid_parts, slope_lower, edges)
    lower_keep, lower_send = weight_grad(pos, act_low_rows, lower_taps, False)
    lower_got = shifted(lower_send, "c", NC, 1)
    own_sum, *sends = core_sum((upper_keep, upper_got), (lower_keep, lower_got))
    lower_taps, _ = lax.optimization_barrier((lower_taps, lower_keep))
    low_part = pl.pallas_call(
        low_kernel,
        out_shape=pltpu.HBM((8, 80, 1024), BF),
        in_specs=[VMEM] * 2,
        out_specs=HBM,
        scratch_shapes=[pltpu.VMEM((8, 80, 1024), BF), pltpu.SemaphoreType.DMA((4,))],
        compiler_params=PARAMS,
        name="low",
    )(lower_taps, lower_full)
    low_part, _ = lax.optimization_barrier((low_part, lower_got))
    low_parts = lax.all_to_all(low_part, DP, split_axis=0, concat_axis=0, tiled=True)
    got = [shifted(sends[s], "y", NY, s + 1) for s in (1, 0, 2)]
    low_grad = pl.pallas_call(
        total_kernel,
        out_shape=jax.ShapeDtypeStruct((80, 1024), BF),
        in_specs=[VMEM],
        out_specs=VMEM,
        compiler_params=PARAMS,
        name="low_total",
    )(low_parts)
    scales = tuple(1.0 / math.sqrt(act.shape[0] * NZ * NY * NC) for act in (act_mid, act_low))
    low_grad, grad_upper, grad_lower = z_sum(own_sum, got, low_grad, scales, weight_upper.shape, weight_lower.shape)
    return low_grad.T, grad_upper, grad_lower


def solution(mesh):
    fine = Mesh(mesh.devices.reshape(4, 2, NZ, NY, NC), DP + SEQ)
    in_specs = (
        P(None, DP + SEQ),
        P(SEQ, None),
        P(SEQ, DP),
        P(SEQ, None),
        P(SEQ, DP),
        P(None, SEQ, DP),
        P(None, SEQ, DP),
    )
    out_specs = (P(SEQ, DP), P(None, SEQ, DP), P(None, SEQ, DP))
    return jax.shard_map(local, mesh=fine, in_specs=in_specs, out_specs=out_specs, check_vma=False)
```
